128 devices in a mesh: layer: 4 (over y_hi, core), lat: 32 (over x, y_lo, z).
Axes of the slice: x: 4, y: 4 (y_hi: 2, y_lo: 2; y = y_hi * 2 + y_lo), z: 4, core: 2. Of those that a mesh axis runs over, the one named last changes fastest.
Arguments:
- resid_halves: bfloat16 [4, 1024, 4096], P('layer'), may hold values from -6 to 6
- enc_weight: bfloat16 [4, 4096, 16384], P('layer', None, 'lat'), may hold values from -0.0625 to 0.0625
- enc_bias: float32 [2, 16384], P(None, 'lat'), may hold values from -3 to 3
- jump_threshold: float32 [2, 16384], P(None, 'lat'), may hold values from 0.1 to 1
- dec_weight: bfloat16 [4, 2, 16384, 8192], P('layer', None, 'lat'), may hold values from -0.03125 to 0.03125
- dec_bias: float32 [4, 8192], P('layer'), may hold values from -3 to 3
- clamp_rows: int32 [2, 1024], replicated, may hold values from 0 to 1023, each once within a row
- clamp_feats: int32 [2, 1024], replicated, may hold values from 0 to 16383
- clamp_slots: int32 [2, 1024], replicated, may hold values from 0 to 15
- clamp_values: float32 [16], replicated, may hold values from 5 to 15
Outputs:
- recon: bfloat16 [4, 1024, 8192], P('layer', 'lat')
The draws below stay inside these ranges and needn't reach their ends.
Inputs may be any that keep to these rules, and one draw needn't show every extreme that they name: Each row of clamp_rows names every token row once.
All inputs are finite; a program needn't handle non-finite values.
Results may differ from the reference program's by a relative error of at most 0.0042.
Values may be sent and summed in bfloat16 or wider, within the bound.
No kernel may reach another device: no remote copies, remote signals or barrier semaphores. Data moves between devices by JAX's collectives and lax.ppermute only.
A program may use at most 192 MiB of HBM per device.

```python
import math
import jax
import jax.numpy as jnp

D = 8192
DH = 4096
LAT = 16384
TOK = 1024
NV = 16


def touch_ends(entries, stream_key, least, top_value):
    shape = entries.shape
    spot = [jax.random.randint(jax.random.fold_in(stream_key, axis), (), 0, shape[axis]) for axis in range(len(shape))]
    entries = entries.at[tuple(spot)].set(least)
    longest = shape.index(max(shape))
    spot[longest] = (spot[longest] + 1) % shape[longest]
    return entries.at[tuple(spot)].set(top_value)


def block_levels(stream_key, shape, pieces, low, largest):
    def one(dim, shards_of):
        draws = jax.random.uniform(jax.random.fold_in(jax.random.fold_in(stream_key, 6), dim), (shards_of,), jnp.float32, low / len(pieces), largest / len(pieces))
        return jnp.repeat(jnp.exp(draws), shape[dim] // shards_of).reshape((-1,) + (1,) * (len(shape) - dim - 1))

    level = one(*pieces[0])
    for cut in pieces[1:]:
        level = level * one(*cut)
    return level


def bell_draw(stream_key, shape, spread, reach, shards=(), dtype=jnp.bfloat16):
    array = spread * jax.random.normal(stream_key, shape, jnp.float32)
    if shards:
        array = array * block_levels(stream_key, shape, shards, -0.22, 0.18)
    return jnp.clip(array, -reach, reach).astype(dtype)


def setup_inputs(seed: int = 0) -> dict:
    key_of = jax.random.split(jax.random.key(seed), 11)
    return {
        "resid_halves": bell_draw(key_of[0], (4, TOK, DH), 1.0, 6.0, ((0, 4),)),
        "enc_weight": bell_draw(key_of[1], (4, DH, LAT), D ** -0.5, 0.0625, ((0, 4), (2, 32))),
        "enc_bias": bell_draw(key_of[2], (2, LAT), 0.5, 3.0, ((1, 32),), jnp.float32),
        "jump_threshold": jnp.clip(jnp.exp(math.log(1.0) - 2.3025851 * jax.random.uniform(key_of[3], (2, LAT), jnp.float32) ** block_levels(key_of[3], (2, LAT), ((1, 32),), -0.2, 0.2)), 0.1, 1.0),
        "dec_weight": bell_draw(key_of[4], (4, 2, LAT, D), (2 * LAT) ** -0.5, 0.03125, ((0, 4), (2, 32))),
        "dec_bias": bell_draw(key_of[5], (4, D), 0.5, 3.0, ((0, 4),), jnp.float32),
        "clamp_rows": jax.vmap(lambda own: jax.random.permutation(own, TOK))(jax.random.split(key_of[6], 2)).reshape((2, TOK)).astype(jnp.int32),
        "clamp_feats": touch_ends(jax.random.randint(key_of[7], (2, TOK), 0, LAT), jax.random.fold_in(key_of[7], 1), 0, LAT - 1).astype(jnp.int32),
        "clamp_slots": touch_ends(jax.random.randint(key_of[8], (2, TOK), 0, NV), jax.random.fold_in(key_of[8], 1), 0, NV - 1).astype(jnp.int32),
        "clamp_values": jnp.clip(jax.random.uniform(key_of[9], (NV,), jnp.float32, 5.0, 15.0), 5.0, 15.0),
    }


def reference(resid_halves, enc_weight, enc_bias, jump_threshold, dec_weight, dec_bias, clamp_rows, clamp_feats, clamp_slots, clamp_values):
    code_list = []
    for source in range(2):
        inputs = jnp.concatenate([resid_halves[2 * source], resid_halves[2 * source + 1]], axis=1)
        weights = jnp.concatenate([enc_weight[2 * source], enc_weight[2 * source + 1]], axis=0)
        pre_act = jnp.dot(inputs, weights, preferred_element_type=jnp.float32) + enc_bias[source][None, :]
        ramp = jnp.clip((pre_act - jump_threshold[source][None, :]) / 0.25 + 1.0, 0.0, 1.0)
        activity = pre_act * ramp
        chosen = clamp_values[clamp_slots[source]]
        activity = activity.at[clamp_rows[source], clamp_feats[source]].set(chosen)
        code_list.append(activity.astype(jnp.bfloat16))
    outputs = []
    for target in range(4):
        total = jnp.dot(code_list[0], dec_weight[target, 0], preferred_element_type=jnp.float32)
        total = total + jnp.dot(code_list[1], dec_weight[target, 1], preferred_element_type=jnp.float32)
        outputs.append((total + dec_bias[target][None, :]).astype(jnp.bfloat16))
    return jnp.stack(outputs, axis=0)
```

```python
import functools

import jax
import jax.numpy as jnp
from jax import lax
from jax.experimental import pallas as pl
from jax.experimental.pallas import tpu as pltpu
from jax.sharding import PartitionSpec as P

BF16, F32 = jnp.bfloat16, jnp.float32
LINKS = (8, 1, 4, 24, 3)
STEPS = len(LINKS)
TILE = 256
PARTS = tuple((p, t) for p, t in zip((0, 1, 2, 3, 4), (7, 7, 6, 6, 6)))


def xor_swap(value, axis, mask):
    return lax.ppermute(value, axis, [(i, i ^ mask) for i in range(lax.axis_size(axis))])


def block_masks():
    n = 1 << STEPS
    out = []
    for j in range(n):
        m = 0
        for k in range(STEPS):
            if (j >> (STEPS - 1 - k)) & 1:
                m ^= LINKS[k]
        out.append(m)
    return out


def part_blocks(first):
    out = []
    for j in range(1 << STEPS):
        base = 0
        for i in range(STEPS):
            if (j >> (STEPS - 1 - i)) & 1:
                base |= 1 << (STEPS - 1 - (first + i) % STEPS)
        out.append(base)
    return out


def encode_kernel(x_hbm, w_hbm, keep_ref, send_ref, xbuf, wbuf, xsem, wsem, *, masks, rows, tile):
    me = lax.axis_index("lat")
    core = lax.axis_index("layer") % 2
    width = w_hbm.shape[2] // 2
    wcopy = pltpu.make_async_copy(w_hbm.at[0], wbuf, wsem)
    wcopy.start()
    copies = []
    for j, mask in enumerate(masks):
        src = jnp.bitwise_xor(me, mask)
        copies.append(
            pltpu.make_async_copy(
                x_hbm.at[0, pl.ds(pl.multiple_of(src * rows, rows), rows)],
                xbuf.at[pl.ds(j * rows, rows)],
                xsem.at[j],
            )
        )
    for c in copies:
        c.start()
    wcopy.wait()
    mine = pl.ds(pl.multiple_of(core * width, width), width)
    other = pl.ds(pl.multiple_of((1 - core) * width, width), width)
    per = tile // rows
    for t in range(len(masks) // per):
        for c in copies[t * per : (t + 1) * per]:
            c.wait()
        at = pl.ds(t * tile, tile)
        send_ref[at, :] = jnp.dot(xbuf[at, :], wbuf[:, other], preferred_element_type=F32)
        keep_ref[at, :] = jnp.dot(xbuf[at, :], wbuf[:, mine], preferred_element_type=F32)


def encode(x, w):
    tokens, depth = x.shape[1], x.shape[2]
    width = w.shape[2] // 2
    masks = block_masks()
    rows = tokens // len(masks)
    half = jax.ShapeDtypeStruct((tokens, width), F32)
    return pl.pallas_call(
        functools.partial(encode_kernel, masks=masks, rows=rows, tile=256),
        out_shape=(half, half),
        in_specs=[pl.BlockSpec(memory_space=pl.ANY)] * 2,
        out_specs=[pl.BlockSpec(memory_space=pltpu.VMEM)] * 2,
        scratch_shapes=[
            pltpu.VMEM((tokens, depth), BF16),
            pltpu.VMEM((depth, 2 * width), BF16),
            pltpu.SemaphoreType.DMA((len(masks),)),
            pltpu.SemaphoreType.DMA,
        ],
        compiler_params=pltpu.CompilerParams(vmem_limit_bytes=28 << 20),
        cost_estimate=pl.CostEstimate(
            flops=4 * tokens * depth * width,
            bytes_accessed=2 * (tokens * depth + 2 * depth * width) + 8 * tokens * width,
            transcendentals=0,
        ),
        name="encode",
    )(x, w)


def decode_kernel(codes_ref, w_ref, keep_ref, send_ref, lhs, *, blocks, rows):
    half = len(blocks) // 2

    @pl.when(pl.program_id(0) == 0)
    def _():
        for j, b in enumerate(blocks):
            lhs[pl.ds(j * rows, rows), :] = codes_ref[pl.ds(b * rows, rows), :]

    n = half * rows
    w = jnp.concatenate([w_ref[0, 0], w_ref[0, 1]], axis=0)
    send_ref[...] = jnp.dot(lhs[n:, :], w, preferred_element_type=F32).astype(BF16)
    keep_ref[...] = jnp.dot(lhs[:n, :], w, preferred_element_type=F32)


def decode(codes, w, first, at, tiles):
    tokens, depth = codes.shape
    blocks = part_blocks(first)
    rows = tokens // len(blocks)
    n = tokens // 2
    wide = tiles * TILE
    return pl.pallas_call(
        functools.partial(decode_kernel, blocks=blocks, rows=rows),
        out_shape=(jax.ShapeDtypeStruct((n, wide), F32), jax.ShapeDtypeStruct((n, wide), BF16)),
        grid=(tiles,),
        in_specs=[
            pl.BlockSpec((tokens, depth), lambda j: (0, 0)),
            pl.BlockSpec((1, 2, depth // 2, TILE), lambda j: (0, 0, 0, at + j)),
        ],
        out_specs=[
            pl.BlockSpec((n, TILE), lambda j: (0, j)),
            pl.BlockSpec((n, TILE), lambda j: (0, j)),
        ],
        scratch_shapes=[pltpu.VMEM((tokens, depth), BF16)],
        compiler_params=pltpu.CompilerParams(vmem_limit_bytes=20 << 20),
        cost_estimate=pl.CostEstimate(
            flops=2 * tokens * depth * wide,
            bytes_accessed=2 * tokens * depth + 2 * depth * wide + 6 * n * wide,
            transcendentals=0,
        ),
        name=f"decode{first}",
    )(codes, w)


def shards(
    resid_halves,
    enc_weight,
    enc_bias,
    jump_threshold,
    dec_weight,
    dec_bias,
    clamp_rows,
    clamp_feats,
    clamp_slots,
    clamp_values,
):
    group = lax.axis_index("layer")
    me = lax.axis_index("lat")
    source, core = group // 2, group % 2
    tokens = resid_halves.shape[1]
    width = enc_weight.shape[2]
    hw = width // 2
    masks = jnp.array(block_masks(), jnp.int32)
    rows = tokens // masks.shape[0]

    keep, send = encode(resid_halves, enc_weight)
    recv = xor_swap(send, "layer", 1)

    row_token = (
        jnp.bitwise_xor(masks, me)[:, None] * rows + jnp.arange(rows, dtype=jnp.int32)[None, :]
    ).reshape(tokens)
    my_rows = lax.dynamic_index_in_dim(clamp_rows, source, 0, keepdims=False)
    my_pick = lax.dynamic_index_in_dim(
        clamp_feats * clamp_values.shape[0] + clamp_slots, source, 0, keepdims=False
    )
    row_hot = (my_rows[:, None] == row_token[None, :]).astype(F32)
    pick = jnp.dot(my_pick.astype(F32), row_hot, precision=lax.Precision.HIGHEST).astype(jnp.int32)
    feat, slot = pick // clamp_values.shape[0], pick % clamp_values.shape[0]
    slot_hot = slot[:, None] == jnp.arange(clamp_values.shape[0], dtype=jnp.int32)[None, :]
    value = jnp.sum(jnp.where(slot_hot, clamp_values[None, :], 0.0), axis=1)
    first = core * hw
    column = feat - me * width - first

    my_bias = lax.dynamic_slice(enc_bias, (source, first), (1, hw))
    my_thresh = lax.dynamic_slice(jump_threshold, (source, first), (1, hw))
    pre = keep + recv + my_bias
    ramp = jnp.clip((pre - my_thresh) / 0.25 + 1.0, 0.0, 1.0)
    hit = column[:, None] == jnp.arange(hw, dtype=jnp.int32)[None, :]
    own = jnp.where(hit, value[:, None], pre * ramp).astype(BF16)

    own_far = xor_swap(own, "layer", 2)
    own_sib = xor_swap(own, "layer", 1)
    far_sib = xor_swap(own_far, "layer", 1)

    def joined(mine, sib):
        return jnp.where(
            core == 0, jnp.concatenate([mine, sib], 1), jnp.concatenate([sib, mine], 1)
        )

    here, there = joined(own, own_sib), joined(own_far, far_sib)
    codes = jnp.where(
        source == 0, jnp.concatenate([here, there], 1), jnp.concatenate([there, here], 1)
    )

    outs, at = [], 0
    for first_link, tiles in PARTS:
        kept, out = decode(codes, dec_weight, first_link, at, tiles)
        for i in range(STEPS):
            got = xor_swap(out, "lat", LINKS[(first_link + i) % STEPS])
            total = kept + got.astype(F32)
            n = total.shape[0] // 2
            kept, out = total[:n], total[n:].astype(BF16)
            if i == STEPS - 1:
                outs.append(total)
        at += tiles
    summed = jnp.concatenate(outs, axis=1)
    return (summed + dec_bias).astype(BF16)[None]


def solution(mesh):
    return jax.shard_map(
        shards,
        mesh=mesh,
        in_specs=(
            P("layer", None, None),
            P("layer", None, "lat"),
            P(None, "lat"),
            P(None, "lat"),
            P("layer", None, "lat", None),
            P("layer", None),
            P(),
            P(),
            P(),
            P(),
        ),
        out_specs=P("layer", "lat", None),
        check_vma=False,
    )
```

```python
import functools

import jax
import jax.numpy as jnp
from jax import lax
from jax.experimental import pallas as pl
from jax.experimental.pallas import tpu as pltpu
from jax.sharding import PartitionSpec as P

BF16, F32 = jnp.bfloat16, jnp.float32
LINKS = (8, 1, 4, 24, 3)
STEPS = len(LINKS)
TILE = 256
PARTS = ((7, 6, 7, 6, 6), (6, 7, 6, 6, 7))
WAVES = len(PARTS)
VMEM = pl.BlockSpec(memory_space=pltpu.VMEM)
HBM = pl.BlockSpec(memory_space=pltpu.HBM)
MIB = 1 << 20


def xor_swap(value, axis, mask):
    return lax.ppermute(value, axis, [(i, i ^ mask) for i in range(lax.axis_size(axis))])


def block_masks():
    n = 1 << STEPS
    out = []
    for j in range(n):
        m = 0
        for k in range(STEPS):
            if (j >> (STEPS - 1 - k)) & 1:
                m ^= LINKS[k]
        out.append(m)
    return out


def part_blocks(first):
    out = []
    for j in range(1 << STEPS):
        base = 0
        for i in range(STEPS):
            if (j >> (STEPS - 1 - i)) & 1:
                base |= 1 << (STEPS - 1 - (first + i) % STEPS)
        out.append(base)
    return out


def encode_kernel(x_hbm, w_hbm, keep_ref, send_ref, xbuf, wbuf, xsem, wsem, *, masks, rows, chunks):
    me = lax.axis_index("lat")
    core = lax.axis_index("layer") % 2
    width = w_hbm.shape[2] // 2
    depth = w_hbm.shape[1] // chunks
    n = len(masks)
    part = rows // WAVES
    wcopies, xcopies = [], []
    for k in range(chunks):
        at = pl.ds(k * depth, depth)
        wcopies.append(pltpu.make_async_copy(w_hbm.at[0, at], wbuf.at[at], wsem.at[k]))
    for h in range(WAVES):
        for j, mask in enumerate(masks):
            src = jnp.bitwise_xor(me, mask) * rows + h * part
            to = (h * n + j) * part
            xcopies.append(
                pltpu.make_async_copy(
                    x_hbm.at[0, pl.ds(pl.multiple_of(src, part), part)],
                    xbuf.at[pl.ds(to, part)],
                    xsem.at[h * n + j],
                )
            )
    for c in wcopies[:1] + xcopies[:n] + wcopies[1:] + xcopies[n:]:
        c.start()
    mine = pl.ds(pl.multiple_of(core * width, width), width)
    other = pl.ds(pl.multiple_of((1 - core) * width, width), width)
    for h in range(WAVES):
        for c in xcopies[h * n : (h + 1) * n]:
            c.wait()
        rs = pl.ds(h * n * part, n * part)
        for k in range(chunks):
            if h == 0:
                wcopies[k].wait()
            at = pl.ds(k * depth, depth)
            x = xbuf[rs, at]
            for ref, cols in ((send_ref, other), (keep_ref, mine)):
                d = jnp.dot(x, wbuf[at, cols], preferred_element_type=F32)
                ref[rs, :] = d if k == 0 else ref[rs, :] + d


def encode(x, w):
    tokens, depth = x.shape[1], x.shape[2]
    width = w.shape[2] // 2
    masks = block_masks()
    rows = tokens // len(masks)
    half = jax.ShapeDtypeStruct((tokens, width), F32)
    return pl.pallas_call(
        functools.partial(encode_kernel, masks=masks, rows=rows, chunks=4),
        out_shape=(half, half),
        in_specs=[HBM, HBM],
        out_specs=[VMEM, VMEM],
        scratch_shapes=[
            pltpu.VMEM((tokens, depth), BF16),
            pltpu.VMEM((depth, 2 * width), BF16),
            pltpu.SemaphoreType.DMA((len(masks) * WAVES,)),
            pltpu.SemaphoreType.DMA((4,)),
        ],
        compiler_params=pltpu.CompilerParams(vmem_limit_bytes=56 * MIB),
        cost_estimate=pl.CostEstimate(
            flops=4 * tokens * depth * width,
            bytes_accessed=2 * (tokens * depth + 2 * depth * width) + 8 * tokens * width,
            transcendentals=0,
        ),
        name="encode",
    )(x, w)


def load_kernel(w_hbm, out, sem, *, pieces):
    step = w_hbm.shape[2] // pieces
    copies = [
        pltpu.make_async_copy(
            w_hbm.at[0, s, pl.ds(q * step, step)], out.at[s, pl.ds(q * step, step)], sem.at[s * pieces + q]
        )
        for s in range(2)
        for q in range(pieces)
    ]
    for c in copies:
        c.start()
    for c in copies:
        c.wait()


def load(w):
    _, sources, depth, wide = w.shape
    return pl.pallas_call(
        functools.partial(load_kernel, pieces=4),
        out_shape=pltpu.VMEM((sources, depth, wide), BF16),
        in_specs=[HBM],
        out_specs=VMEM,
        scratch_shapes=[pltpu.SemaphoreType.DMA((8,))],
        compiler_params=pltpu.CompilerParams(vmem_limit_bytes=40 * MIB),
        cost_estimate=pl.CostEstimate(
            flops=0, bytes_accessed=4 * sources * depth * wide, transcendentals=0
        ),
        name="load",
    )(w)


def assemble_kernel(own_ref, own_sib_ref, far_ref, far_sib_ref, out_ref):
    group = lax.axis_index("layer")
    source, core = group // 2, group % 2
    hw = own_ref.shape[1]
    for ref, s, c in (
        (own_ref, source, core),
        (own_sib_ref, source, 1 - core),
        (far_ref, 1 - source, core),
        (far_sib_ref, 1 - source, 1 - core),
    ):
        out_ref[:, pl.ds(pl.multiple_of((s * 2 + c) * hw, hw), hw)] = ref[...]


def assemble(*pieces):
    n, hw = pieces[0].shape
    return pl.pallas_call(
        assemble_kernel,
        out_shape=pltpu.VMEM((n, 4 * hw), BF16),
        in_specs=[VMEM] * 4,
        out_specs=VMEM,
        compiler_params=pltpu.CompilerParams(vmem_limit_bytes=8 * MIB),
        name="assemble",
    )(*pieces)


def gather_rows(codes_ref, lhs, blocks):
    rows = lhs.shape[0] // len(blocks)
    for j, b in enumerate(blocks):
        lhs[pl.ds(j * rows, rows), :] = codes_ref[pl.ds(b * rows, rows), :]


def tile_product(lhs, w_ref, at, t):
    w = w_ref[:, :, pl.ds(pl.multiple_of(at + t * TILE, TILE), TILE)]
    return jnp.dot(lhs[...], w.reshape(lhs.shape[1], TILE), preferred_element_type=F32)


def send_kernel(codes_ref, w_ref, send_ref, lhs, *, blocks, at):
    gather_rows(codes_ref, lhs, blocks)

    @pl.loop(0, send_ref.shape[1] // TILE)
    def _(t):
        cols = pl.ds(pl.multiple_of(t * TILE, TILE), TILE)
        send_ref[:, cols] = tile_product(lhs, w_ref, at, t).astype(BF16)


def keep_kernel(codes_ref, w_ref, got_ref, keep_ref, send_ref, lhs, *, blocks, at):
    gather_rows(codes_ref, lhs, blocks)
    n2 = lhs.shape[0] // 2

    @pl.loop(0, send_ref.shape[1] // TILE)
    def _(t):
        cols = pl.ds(pl.multiple_of(t * TILE, TILE), TILE)
        total = tile_product(lhs, w_ref, at, t) + got_ref[:, cols].astype(F32)
        keep_ref[:, cols] = total[:n2]
        send_ref[:, cols] = total[n2:].astype(BF16)


def decode_send(codes, w, first, at, wide):
    tokens, depth = codes.shape
    blocks = part_blocks(first)
    n = tokens // 2
    return pl.pallas_call(
        functools.partial(send_kernel, blocks=blocks[len(blocks) // 2 :], at=at),
        out_shape=jax.ShapeDtypeStruct((n, wide), BF16),
        in_specs=[VMEM, VMEM],
        out_specs=VMEM,
        scratch_shapes=[pltpu.VMEM((n, depth), BF16)],
        compiler_params=pltpu.CompilerParams(vmem_limit_bytes=8 * MIB),
        cost_estimate=pl.CostEstimate(flops=1000, bytes_accessed=1000, transcendentals=0),
        name=f"send{first}",
    )(codes, w)


def decode_keep(codes, w, got, first, at, wide):
    tokens, depth = codes.shape
    blocks = part_blocks(first)
    n = tokens // 2
    return pl.pallas_call(
        functools.partial(keep_kernel, blocks=blocks[: len(blocks) // 2], at=at),
        out_shape=(
            jax.ShapeDtypeStruct((n // 2, wide), F32),
            jax.ShapeDtypeStruct((n // 2, wide), BF16),
        ),
        in_specs=[VMEM, VMEM, VMEM],
        out_specs=[VMEM, VMEM],
        scratch_shapes=[pltpu.VMEM((n, depth), BF16)],
        compiler_params=pltpu.CompilerParams(vmem_limit_bytes=8 * MIB),
        cost_estimate=pl.CostEstimate(flops=1000, bytes_accessed=1000, transcendentals=0),
        name=f"keep{first}",
    )(codes, w, got)

def shards(
    resid_halves,
    enc_weight,
    enc_bias,
    jump_threshold,
    dec_weight,
    dec_bias,
    clamp_rows,
    clamp_feats,
    clamp_slots,
    clamp_values,
):
    group = lax.axis_index("layer")
    me = lax.axis_index("lat")
    source, core = group // 2, group % 2
    tokens = resid_halves.shape[1]
    width = enc_weight.shape[2]
    hw = width // 2
    masks = jnp.array(block_masks(), jnp.int32)
    rows = tokens // masks.shape[0]

    keep, send = encode(resid_halves, enc_weight)
    recv = xor_swap(send, "layer", 1)

    part = rows // WAVES
    within = jnp.arange(part, dtype=jnp.int32)
    row_token = (
        (jnp.bitwise_xor(masks, me) * rows)[None, :, None]
        + (jnp.arange(WAVES, dtype=jnp.int32) * part)[:, None, None]
        + within[None, None, :]
    ).reshape(tokens)
    my_rows = lax.dynamic_index_in_dim(clamp_rows, source, 0, keepdims=False)
    my_pick = lax.dynamic_index_in_dim(
        clamp_feats * clamp_values.shape[0] + clamp_slots, source, 0, keepdims=False
    )
    row_hot = (my_rows[:, None] == row_token[None, :]).astype(F32)
    pick = jnp.dot(my_pick.astype(F32), row_hot, precision=lax.Precision.HIGHEST).astype(jnp.int32)
    feat, slot = pick // clamp_values.shape[0], pick % clamp_values.shape[0]
    slot_hot = slot[:, None] == jnp.arange(clamp_values.shape[0], dtype=jnp.int32)[None, :]
    value = jnp.sum(jnp.where(slot_hot, clamp_values[None, :], 0.0), axis=1)
    first = core * hw
    column = feat - me * width - first

    my_bias = lax.dynamic_slice(enc_bias, (source, first), (1, hw))
    my_thresh = lax.dynamic_slice(jump_threshold, (source, first), (1, hw))
    pre = keep + recv + my_bias
    ramp = jnp.clip((pre - my_thresh) / 0.25 + 1.0, 0.0, 1.0)
    hit = column[:, None] == jnp.arange(hw, dtype=jnp.int32)[None, :]
    own = jnp.where(hit, value[:, None], pre * ramp).astype(BF16)

    own_sib = xor_swap(own, "layer", 1)
    weights = load(lax.optimization_barrier((dec_weight, own))[0])
    n = tokens // WAVES
    codes, far = [], None
    for h in range(WAVES):
        mine = own[h * n : (h + 1) * n]
        sent = mine if far is None else lax.optimization_barrier((mine, far, weights))[0]
        far = xor_swap(sent, "layer", 2)
        codes.append(
            assemble(mine, own_sib[h * n : (h + 1) * n], far, xor_swap(far, "layer", 1))
        )

    starts = [[sum(wave[:p]) * TILE for p in range(STEPS)] for wave in PARTS]
    out, kept = {}, {}
    for h in range(WAVES):
        for p in range(STEPS):
            out[h, p] = decode_send(codes[h], weights, p, starts[h][p], PARTS[h][p] * TILE)
    last = [None] * STEPS
    for i in range(STEPS):
        for h in range(WAVES):
            for p in range(STEPS):
                link = (p + i) % STEPS
                data = out[h, p]
                if last[link] is not None:
                    data = lax.optimization_barrier((data, last[link]))[0]
                got = last[link] = xor_swap(data, "lat", LINKS[link])
                if i == 0:
                    kept[h, p], out[h, p] = decode_keep(
                        codes[h], weights, got, p, starts[h][p], PARTS[h][p] * TILE
                    )
                else:
                    total = kept[h, p] + got.astype(F32)
                    m = total.shape[0] // 2
                    kept[h, p] = total[:m] if i < STEPS - 1 else total
                    out[h, p] = total[m:].astype(BF16)
    summed = [jnp.concatenate([kept[h, p] for p in range(STEPS)], axis=1) for h in range(WAVES)]
    return (jnp.concatenate(summed, axis=0) + dec_bias).astype(BF16)[None]


def solution(mesh):
    return jax.shard_map(
        shards,
        mesh=mesh,
        in_specs=(
            P("layer", None, None),
            P("layer", None, "lat"),
            P(None, "lat"),
            P(None, "lat"),
            P("layer", None, "lat", None),
            P("layer", None),
            P(),
            P(),
            P(),
            P(),
        ),
        out_specs=P("layer", "lat", None),
        check_vma=False,
    )
```

```python
import functools

import jax
import jax.numpy as jnp
from jax import lax
from jax.experimental import pallas as pl
from jax.experimental.pallas import tpu as pltpu
from jax.sharding import PartitionSpec as P

BF16, F32 = jnp.bfloat16, jnp.float32
LINKS = (8, 1, 4, 24, 3)
STEPS = len(LINKS)
LANES, TILE = 128, 256
PARTS = (12, 13, 13, 13, 13)
EARLY = (6, 6, 6, 6, 6)
VMEM = pl.BlockSpec(memory_space=pltpu.VMEM)
HBM = pl.BlockSpec(memory_space=pltpu.HBM)
MIB = 1 << 20


def xor_swap(value, axis, mask):
    return lax.ppermute(value, axis, [(i, i ^ mask) for i in range(lax.axis_size(axis))])


def block_masks():
    n = 1 << STEPS
    out = []
    for j in range(n):
        m = 0
        for k in range(STEPS):
            if (j >> (STEPS - 1 - k)) & 1:
                m ^= LINKS[k]
        out.append(m)
    return out


def part_blocks(first):
    out = []
    for j in range(1 << STEPS):
        base = 0
        for i in range(STEPS):
            if (j >> (STEPS - 1 - i)) & 1:
                base |= 1 << (STEPS - 1 - (first + i) % STEPS)
        out.append(base)
    return out


def encode_kernel(
    x_hbm, w_hbm, keep_ref, send_ref, xbuf, wbuf, xsem, wsem, *, masks, rows, chunks
):
    me = lax.axis_index("lat")
    core = lax.axis_index("layer") % 2
    width = w_hbm.shape[2] // 2
    copies = []
    for k, (at, depth) in enumerate(chunks):
        ks = pl.ds(at, depth)
        mine = [pltpu.make_async_copy(w_hbm.at[0, ks], wbuf.at[ks], wsem.at[k])]
        for j, mask in enumerate(masks):
            src = pl.multiple_of(jnp.bitwise_xor(me, mask) * rows, rows)
            mine.append(
                pltpu.make_async_copy(
                    x_hbm.at[0, pl.ds(src, rows), ks],
                    xbuf.at[pl.ds(j * rows, rows), ks],
                    xsem.at[k * len(masks) + j],
                )
            )
        copies.append(mine)
    for mine in copies:
        for c in mine:
            c.start()
    half = (
        pl.ds(pl.multiple_of((1 - core) * width, width), width),
        pl.ds(pl.multiple_of(core * width, width), width),
    )
    for k, (at, depth) in enumerate(chunks):
        for c in copies[k]:
            c.wait()
        ks = pl.ds(at, depth)
        for ref, cols in zip((send_ref, keep_ref), half):
            d = jnp.dot(xbuf[:, ks], wbuf[ks, cols], preferred_element_type=F32)
            ref[...] = d if k == 0 else ref[...] + d


def encode(x, w):
    tokens, depth = x.shape[1], x.shape[2]
    width = w.shape[2] // 2
    masks = block_masks()
    rows = tokens // len(masks)
    q = depth // 4
    chunks = ((0, q), (q, q), (2 * q, 2 * q))
    half = pltpu.VMEM((tokens, width), F32)
    return pl.pallas_call(
        functools.partial(encode_kernel, masks=masks, rows=rows, chunks=chunks),
        out_shape=(half, half),
        in_specs=[HBM] * 2,
        out_specs=[VMEM] * 2,
        scratch_shapes=[
            pltpu.VMEM((tokens, depth), BF16),
            pltpu.VMEM((depth, 2 * width), BF16),
            pltpu.SemaphoreType.DMA((len(masks) * len(chunks),)),
            pltpu.SemaphoreType.DMA((len(chunks),)),
        ],
        compiler_params=pltpu.CompilerParams(vmem_limit_bytes=54 * MIB),
        cost_estimate=pl.CostEstimate(
            flops=4 * tokens * depth * width,
            bytes_accessed=2 * (tokens * depth + 2 * depth * width) + 8 * tokens * width,
            transcendentals=0,
        ),
        name="encode",
    )(x, w)


def load_kernel(w_hbm, out, sem, *, pieces):
    step = w_hbm.shape[2] // pieces
    copies = [
        pltpu.make_async_copy(
            w_hbm.at[0, s, pl.ds(q * step, step)], out.at[s, pl.ds(q * step, step)], sem.at[s * pieces + q]
        )
        for s in range(2)
        for q in range(pieces)
    ]
    for c in copies:
        c.start()
    for c in copies:
        c.wait()


def load(w):
    _, sources, depth, wide = w.shape
    return pl.pallas_call(
        functools.partial(load_kernel, pieces=4),
        out_shape=pltpu.VMEM((sources, depth, wide), BF16),
        in_specs=[HBM],
        out_specs=VMEM,
        scratch_shapes=[pltpu.SemaphoreType.DMA((8,))],
        compiler_params=pltpu.CompilerParams(vmem_limit_bytes=40 * MIB),
        cost_estimate=pl.CostEstimate(
            flops=0, bytes_accessed=4 * sources * depth * wide, transcendentals=0
        ),
        name="load",
    )(w)


def assemble_kernel(own_ref, own_sib_ref, far_ref, far_sib_ref, out_ref):
    group = lax.axis_index("layer")
    source, core = group // 2, group % 2
    hw = own_ref.shape[1]
    for ref, s, c in (
        (own_ref, source, core),
        (own_sib_ref, source, 1 - core),
        (far_ref, 1 - source, core),
        (far_sib_ref, 1 - source, 1 - core),
    ):
        out_ref[:, pl.ds(pl.multiple_of((s * 2 + c) * hw, hw), hw)] = ref[...]


def assemble(*pieces):
    n, hw = pieces[0].shape
    return pl.pallas_call(
        assemble_kernel,
        out_shape=pltpu.VMEM((n, 4 * hw), BF16),
        in_specs=[VMEM] * 4,
        out_specs=VMEM,
        compiler_params=pltpu.CompilerParams(vmem_limit_bytes=8 * MIB),
        name="assemble",
    )(*pieces)


def gather_rows(codes_ref, lhs, blocks):
    rows = lhs.shape[0] // len(blocks)
    for j, b in enumerate(blocks):
        lhs[pl.ds(j * rows, rows), :] = codes_ref[pl.ds(b * rows, rows), :]


def over_tiles(begin, end, body):
    whole = (end - begin) // TILE

    @pl.loop(0, whole)
    def _(t):
        body(pl.multiple_of(begin + t * TILE, LANES), TILE)

    if begin + whole * TILE < end:
        body(begin + whole * TILE, end - begin - whole * TILE)


def product(lhs, w_ref, at, n):
    w = w_ref[:, :, pl.ds(pl.multiple_of(at, LANES), n)]
    return jnp.dot(lhs[...], w.reshape(lhs.shape[1], n), preferred_element_type=F32)


def send_kernel(codes_ref, w_ref, send_ref, lhs, *, blocks, at):
    gather_rows(codes_ref, lhs, blocks)

    def body(c, n):
        send_ref[:, pl.ds(c, n)] = product(lhs, w_ref, at + c, n).astype(BF16)

    over_tiles(0, send_ref.shape[1], body)


def keep_kernel(codes_ref, w_ref, early_ref, late_ref, keep_ref, send_ref, lhs, *, blocks, at):
    gather_rows(codes_ref, lhs, blocks)
    m = lhs.shape[0] // 2
    split = early_ref.shape[1]
    for got_ref, begin, end in ((early_ref, 0, split), (late_ref, split, send_ref.shape[1])):

        def body(c, n):
            got = got_ref[:, pl.ds(pl.multiple_of(c - begin, LANES), n)]
            total = product(lhs, w_ref, at + c, n) + got.astype(F32)
            keep_ref[:, pl.ds(c, n)] = total[:m]
            send_ref[:, pl.ds(c, n)] = total[m:].astype(BF16)

        over_tiles(begin, end, body)


def decode_send(codes, w, first, at, wide):
    tokens, depth = codes.shape
    blocks = part_blocks(first)
    n = tokens // 2
    return pl.pallas_call(
        functools.partial(send_kernel, blocks=blocks[len(blocks) // 2 :], at=at),
        out_shape=jax.ShapeDtypeStruct((n, wide), BF16),
        in_specs=[VMEM, VMEM],
        out_specs=VMEM,
        scratch_shapes=[pltpu.VMEM((n, depth), BF16)],
        compiler_params=pltpu.CompilerParams(vmem_limit_bytes=8 * MIB),
        cost_estimate=pl.CostEstimate(flops=1000, bytes_accessed=1000, transcendentals=0),
        name=f"send{first}",
    )(codes, w)


def decode_keep(codes, w, early, late, first, at):
    tokens, depth = codes.shape
    blocks = part_blocks(first)
    n = tokens // 2
    wide = early.shape[1] + late.shape[1]
    return pl.pallas_call(
        functools.partial(keep_kernel, blocks=blocks[: len(blocks) // 2], at=at),
        out_shape=(
            jax.ShapeDtypeStruct((n // 2, wide), F32),
            jax.ShapeDtypeStruct((n // 2, wide), BF16),
        ),
        in_specs=[VMEM] * 4,
        out_specs=[VMEM, VMEM],
        scratch_shapes=[pltpu.VMEM((n, depth), BF16)],
        compiler_params=pltpu.CompilerParams(vmem_limit_bytes=8 * MIB),
        cost_estimate=pl.CostEstimate(flops=1000, bytes_accessed=1000, transcendentals=0),
        name=f"keep{first}",
    )(codes, w, early, late)


def shards(
    resid_halves,
    enc_weight,
    enc_bias,
    jump_threshold,
    dec_weight,
    dec_bias,
    clamp_rows,
    clamp_feats,
    clamp_slots,
    clamp_values,
):
    group = lax.axis_index("layer")
    me = lax.axis_index("lat")
    source, core = group // 2, group % 2
    tokens = resid_halves.shape[1]
    width = enc_weight.shape[2]
    hw = width // 2
    masks = jnp.array(block_masks(), jnp.int32)
    rows = tokens // masks.shape[0]

    keep, send = encode(resid_halves, enc_weight)
    recv = xor_swap(send, "layer", 1)

    row_token = (
        jnp.bitwise_xor(masks, me)[:, None] * rows + jnp.arange(rows, dtype=jnp.int32)[None, :]
    ).reshape(tokens)
    my_rows = lax.dynamic_index_in_dim(clamp_rows, source, 0, keepdims=False)
    my_pick = lax.dynamic_index_in_dim(
        clamp_feats * clamp_values.shape[0] + clamp_slots, source, 0, keepdims=False
    )
    row_hot = (my_rows[:, None] == row_token[None, :]).astype(F32)
    pick = jnp.dot(my_pick.astype(F32), row_hot, precision=lax.Precision.HIGHEST).astype(jnp.int32)
    feat, slot = pick // clamp_values.shape[0], pick % clamp_values.shape[0]
    slot_hot = slot[:, None] == jnp.arange(clamp_values.shape[0], dtype=jnp.int32)[None, :]
    value = jnp.sum(jnp.where(slot_hot, clamp_values[None, :], 0.0), axis=1)
    first = core * hw
    column = feat - me * width - first

    my_bias = lax.dynamic_slice(enc_bias, (source, first), (1, hw))
    my_thresh = lax.dynamic_slice(jump_threshold, (source, first), (1, hw))
    pre = keep + recv + my_bias
    ramp = jnp.clip((pre - my_thresh) / 0.25 + 1.0, 0.0, 1.0)
    hit = column[:, None] == jnp.arange(hw, dtype=jnp.int32)[None, :]
    own = jnp.where(hit, value[:, None], pre * ramp).astype(BF16)

    own_sib = xor_swap(own, "layer", 1)

    weights = load(lax.optimization_barrier((dec_weight, own))[0])
    far, weights = lax.optimization_barrier((xor_swap(own, "layer", 2), weights))
    codes = assemble(own, own_sib, far, xor_swap(far, "layer", 1))

    starts = [sum(PARTS[:p]) * LANES for p in range(STEPS)]
    last = [None] * STEPS

    def exchange(data, link):
        if last[link] is not None:
            data = lax.optimization_barrier((data, last[link]))[0]
        last[link] = xor_swap(data, "lat", LINKS[link])
        return last[link]

    got = [[] for _ in PARTS]
    for late in (False, True):
        for p in range(STEPS):
            at, wide = starts[p], EARLY[p] * LANES
            if late:
                at, wide = at + wide, PARTS[p] * LANES - wide
            got[p].append(exchange(decode_send(codes, weights, p, at, wide), p))
    kept, out = {}, {}
    for p in range(STEPS):
        kept[p], out[p] = decode_keep(codes, weights, *got[p], p, starts[p])
    for i in range(1, STEPS):
        for p in range(STEPS):
            total = kept[p] + exchange(out[p], (p + i) % STEPS).astype(F32)
            m = total.shape[0] // 2
            kept[p] = total[:m] if i < STEPS - 1 else total
            out[p] = total[m:].astype(BF16)
    summed = jnp.concatenate([kept[p] for p in range(STEPS)], axis=1)
    return (summed + dec_bias).astype(BF16)[None]


def solution(mesh):
    return jax.shard_map(
        shards,
        mesh=mesh,
        in_specs=(
            P("layer", None, None),
            P("layer", None, "lat"),
            P(None, "lat"),
            P(None, "lat"),
            P("layer", None, "lat", None),
            P("layer", None),
            P(),
            P(),
            P(),
            P(),
        ),
        out_specs=P("layer", "lat", None),
        check_vma=False,
    )
```

```python
import functools

import jax
import jax.numpy as jnp
from jax import lax
from jax.experimental import pallas as pl
from jax.experimental.pallas import tpu as pltpu
from jax.sharding import PartitionSpec as P

BF16, F32 = jnp.bfloat16, jnp.float32
LINKS = (8, 1, 4, 24, 3)
STEPS = len(LINKS)
LANES, TILE = 128, 256
PARTS = (12, 13, 13, 13, 13)
EARLY = (6, 6, 6, 6, 6)
VMEM = pl.BlockSpec(memory_space=pltpu.VMEM)
HBM = pl.BlockSpec(memory_space=pltpu.HBM)
MIB = 1 << 20
COPIES = 4


def xor_swap(value, axis, mask):
    return lax.ppermute(value, axis, [(i, i ^ mask) for i in range(lax.axis_size(axis))])


def block_masks():
    n = 1 << STEPS
    out = []
    for j in range(n):
        m = 0
        for k in range(STEPS):
            if (j >> (STEPS - 1 - k)) & 1:
                m ^= LINKS[k]
        out.append(m)
    return out


def part_blocks(first):
    out = []
    for j in range(1 << STEPS):
        base = 0
        for i in range(STEPS):
            if (j >> (STEPS - 1 - i)) & 1:
                base |= 1 << (STEPS - 1 - (first + i) % STEPS)
        out.append(base)
    return out


def encode_kernel(
    x_hbm, w_hbm, keep_ref, send_ref, xbuf, wbuf, xsem, wsem, *, masks, rows, chunks
):
    me = lax.axis_index("lat")
    core = lax.axis_index("layer") % 2
    width = w_hbm.shape[2] // 2
    copies = []
    for k, (at, depth) in enumerate(chunks):
        ks = pl.ds(at, depth)
        mine = [pltpu.make_async_copy(w_hbm.at[0, ks], wbuf.at[ks], wsem.at[k])]
        for j, mask in enumerate(masks):
            src = pl.multiple_of(jnp.bitwise_xor(me, mask) * rows, rows)
            mine.append(
                pltpu.make_async_copy(
                    x_hbm.at[0, pl.ds(src, rows), ks],
                    xbuf.at[pl.ds(j * rows, rows), ks],
                    xsem.at[k * len(masks) + j],
                )
            )
        copies.append(mine)
    for mine in copies:
        for c in mine:
            c.start()
    half = (
        pl.ds(pl.multiple_of((1 - core) * width, width), width),
        pl.ds(pl.multiple_of(core * width, width), width),
    )
    for k, (at, depth) in enumerate(chunks):
        for c in copies[k]:
            c.wait()
        ks = pl.ds(at, depth)
        for ref, cols in zip((send_ref, keep_ref), half):
            d = jnp.dot(xbuf[:, ks], wbuf[ks, cols], preferred_element_type=F32)
            ref[...] = d if k == 0 else ref[...] + d


def encode(x, w):
    tokens, depth = x.shape[1], x.shape[2]
    width = w.shape[2] // 2
    masks = block_masks()
    rows = tokens // len(masks)
    q = depth // 4
    chunks = ((0, q), (q, q), (2 * q, 2 * q))
    half = pltpu.VMEM((tokens, width), F32)
    return pl.pallas_call(
        functools.partial(encode_kernel, masks=masks, rows=rows, chunks=chunks),
        out_shape=(half, half),
        in_specs=[HBM] * 2,
        out_specs=[VMEM] * 2,
        scratch_shapes=[
            pltpu.VMEM((tokens, depth), BF16),
            pltpu.VMEM((depth, 2 * width), BF16),
            pltpu.SemaphoreType.DMA((len(masks) * len(chunks),)),
            pltpu.SemaphoreType.DMA((len(chunks),)),
        ],
        compiler_params=pltpu.CompilerParams(vmem_limit_bytes=54 * MIB),
        cost_estimate=pl.CostEstimate(
            flops=4 * tokens * depth * width,
            bytes_accessed=2 * (tokens * depth + 2 * depth * width) + 8 * tokens * width,
            transcendentals=0,
        ),
        name="encode",
    )(x, w)


def copy_weights(dec_hbm, source, out_ref, sem, start):
    step = out_ref.shape[0] // COPIES
    for q in range(COPIES):
        at = pl.ds(q * step, step)
        c = pltpu.make_async_copy(dec_hbm.at[0, source, at], out_ref.at[at], sem.at[q])
        if start:
            c.start()
        else:
            c.wait()


def join_kernel(mine_ref, sib_ref, out_ref):
    core = lax.axis_index("layer") % 2
    hw = mine_ref.shape[1]
    out_ref[:, pl.ds(pl.multiple_of(core * hw, hw), hw)] = mine_ref[...]
    out_ref[:, pl.ds(pl.multiple_of((1 - core) * hw, hw), hw)] = sib_ref[...]


def join(mine, sib):
    n, hw = mine.shape
    return pl.pallas_call(
        join_kernel,
        out_shape=pltpu.VMEM((n, 2 * hw), BF16),
        in_specs=[VMEM] * 2,
        out_specs=VMEM,
        compiler_params=pltpu.CompilerParams(vmem_limit_bytes=8 * MIB),
        name="join",
    )(mine, sib)


def gather_rows(codes_ref, lhs, blocks):
    rows = lhs.shape[0] // len(blocks)
    for j, b in enumerate(blocks):
        lhs[pl.ds(j * rows, rows), :] = codes_ref[pl.ds(b * rows, rows), :]


def over_tiles(begin, end, body):
    whole = (end - begin) // TILE

    @pl.loop(0, whole)
    def _(t):
        body(pl.multiple_of(begin + t * TILE, LANES), TILE)

    if begin + whole * TILE < end:
        body(begin + whole * TILE, end - begin - whole * TILE)


def product(lhs, w_ref, at, n):
    w = w_ref[:, pl.ds(pl.multiple_of(at, LANES), n)]
    return jnp.dot(lhs[...], w, preferred_element_type=F32)


def own_kernel(mine_ref, sib_ref, dec_hbm, *refs, spans):
    codes_ref, w_ref, far_ref, *accs = refs[: 3 + len(spans)]
    lhs, w_sem, far_sem = refs[3 + len(spans) :]
    source = lax.axis_index("layer") // 2
    copy_weights(dec_hbm, source, w_ref, w_sem, True)
    copy_weights(dec_hbm, 1 - source, far_ref, far_sem, True)
    join_kernel(mine_ref, sib_ref, codes_ref)
    copy_weights(dec_hbm, source, w_ref, w_sem, False)
    done = None
    for (part, at, wide), acc in zip(spans, accs):
        if part != done:
            gather_rows(codes_ref, lhs, send_blocks(part))
            done = part

        def body(c, n):
            acc[:, pl.ds(c, n)] = product(lhs, w_ref, at + c, n)

        over_tiles(0, wide, body)
    copy_weights(dec_hbm, 1 - source, far_ref, far_sem, False)


def own_part(mine, sib, dec, spans):
    tokens, hw = mine.shape
    _, _, depth, wide = dec.shape
    n = tokens // 2
    codes, w_own, w_far, *accs = pl.pallas_call(
        functools.partial(own_kernel, spans=spans),
        out_shape=[pltpu.VMEM((tokens, 2 * hw), BF16)]
        + [pltpu.VMEM((depth, wide), BF16)] * 2
        + [pltpu.VMEM((n, span[2]), F32) for span in spans],
        in_specs=[VMEM, VMEM, HBM],
        out_specs=[VMEM] * (3 + len(spans)),
        scratch_shapes=[pltpu.VMEM((n, depth), BF16)] + [pltpu.SemaphoreType.DMA((COPIES,))] * 2,
        compiler_params=pltpu.CompilerParams(vmem_limit_bytes=14 * MIB),
        cost_estimate=pl.CostEstimate(
            flops=2 * n * depth * wide, bytes_accessed=4 * depth * wide, transcendentals=0
        ),
        name="own",
    )(mine, sib, dec)
    return codes, w_own, w_far, accs


def send_blocks(part):
    blocks = part_blocks(part)
    return blocks[len(blocks) // 2 :]


def keep_blocks(part):
    blocks = part_blocks(part)
    return blocks[: len(blocks) // 2]


def send_kernel(codes_ref, w_ref, acc_ref, send_ref, lhs, *, blocks, at):
    gather_rows(codes_ref, lhs, blocks)

    def body(c, n):
        cols = pl.ds(c, n)
        send_ref[:, cols] = (acc_ref[:, cols] + product(lhs, w_ref, at + c, n)).astype(BF16)

    over_tiles(0, send_ref.shape[1], body)


def decode_send(codes, w, acc, part, at):
    n, wide = acc.shape
    return pl.pallas_call(
        functools.partial(send_kernel, blocks=send_blocks(part), at=at),
        out_shape=jax.ShapeDtypeStruct((n, wide), BF16),
        in_specs=[VMEM] * 3,
        out_specs=VMEM,
        scratch_shapes=[pltpu.VMEM((n, codes.shape[1]), BF16)],
        compiler_params=pltpu.CompilerParams(vmem_limit_bytes=6 * MIB),
        cost_estimate=pl.CostEstimate(flops=1000, bytes_accessed=1000, transcendentals=0),
        name=f"send{part}",
    )(codes, w, acc)


def keep_kernel(own_ref, far_ref, w_own_ref, w_far_ref, keep_ref, own_lhs, far_lhs, *, blocks, at):
    gather_rows(own_ref, own_lhs, blocks)
    gather_rows(far_ref, far_lhs, blocks)

    def body(c, n):
        keep_ref[:, pl.ds(c, n)] = product(own_lhs, w_own_ref, at + c, n) + product(
            far_lhs, w_far_ref, at + c, n
        )

    over_tiles(0, keep_ref.shape[1], body)


def decode_keep(own, far, w_own, w_far, part, at, wide):
    tokens, depth = own.shape
    n = tokens // 2
    return pl.pallas_call(
        functools.partial(keep_kernel, blocks=keep_blocks(part), at=at),
        out_shape=jax.ShapeDtypeStruct((n, wide), F32),
        in_specs=[VMEM] * 4,
        out_specs=VMEM,
        scratch_shapes=[pltpu.VMEM((n, depth), BF16)] * 2,
        compiler_params=pltpu.CompilerParams(vmem_limit_bytes=8 * MIB),
        cost_estimate=pl.CostEstimate(flops=1000, bytes_accessed=1000, transcendentals=0),
        name=f"keep{part}",
    )(own, far, w_own, w_far)


def merge_kernel(keep_ref, early_ref, late_ref, new_ref, send_ref):
    m = new_ref.shape[0]
    split = early_ref.shape[1]
    for got, cols in ((early_ref, pl.ds(0, split)), (late_ref, pl.ds(split, late_ref.shape[1]))):
        new_ref[:, cols] = keep_ref[:m, cols] + got[:m, :].astype(F32)
        send_ref[:, cols] = (keep_ref[m:, cols] + got[m:, :].astype(F32)).astype(BF16)


def merge(keep, early, late):
    n, wide = keep.shape
    return pl.pallas_call(
        merge_kernel,
        out_shape=(
            jax.ShapeDtypeStruct((n // 2, wide), F32),
            jax.ShapeDtypeStruct((n // 2, wide), BF16),
        ),
        in_specs=[VMEM] * 3,
        out_specs=[VMEM] * 2,
        compiler_params=pltpu.CompilerParams(vmem_limit_bytes=8 * MIB),
        cost_estimate=pl.CostEstimate(flops=1000, bytes_accessed=1000, transcendentals=0),
        name="merge",
    )(keep, early, late)


def shards(
    resid_halves,
    enc_weight,
    enc_bias,
    jump_threshold,
    dec_weight,
    dec_bias,
    clamp_rows,
    clamp_feats,
    clamp_slots,
    clamp_values,
):
    group = lax.axis_index("layer")
    me = lax.axis_index("lat")
    source, core = group // 2, group % 2
    tokens = resid_halves.shape[1]
    width = enc_weight.shape[2]
    hw = width // 2
    masks = jnp.array(block_masks(), jnp.int32)
    rows = tokens // masks.shape[0]

    keep, send = encode(resid_halves, enc_weight)
    recv = xor_swap(send, "layer", 1)

    row_token = (
        jnp.bitwise_xor(masks, me)[:, None] * rows + jnp.arange(rows, dtype=jnp.int32)[None, :]
    ).reshape(tokens)
    my_rows = lax.dynamic_index_in_dim(clamp_rows, source, 0, keepdims=False)
    my_pick = lax.dynamic_index_in_dim(
        clamp_feats * clamp_values.shape[0] + clamp_slots, source, 0, keepdims=False
    )
    row_hot = (my_rows[:, None] == row_token[None, :]).astype(F32)
    pick = jnp.dot(my_pick.astype(F32), row_hot, precision=lax.Precision.HIGHEST).astype(jnp.int32)
    feat, slot = pick // clamp_values.shape[0], pick % clamp_values.shape[0]
    slot_hot = slot[:, None] == jnp.arange(clamp_values.shape[0], dtype=jnp.int32)[None, :]
    value = jnp.sum(jnp.where(slot_hot, clamp_values[None, :], 0.0), axis=1)
    first = core * hw
    column = feat - me * width - first

    my_bias = lax.dynamic_slice(enc_bias, (source, first), (1, hw))
    my_thresh = lax.dynamic_slice(jump_threshold, (source, first), (1, hw))
    pre = keep + recv + my_bias
    ramp = jnp.clip((pre - my_thresh) / 0.25 + 1.0, 0.0, 1.0)
    hit = column[:, None] == jnp.arange(hw, dtype=jnp.int32)[None, :]
    own = jnp.where(hit, value[:, None], pre * ramp).astype(BF16)

    own_sib = xor_swap(own, "layer", 1)

    starts = [sum(PARTS[:p]) * LANES for p in range(STEPS)]
    spans = []
    for late in (False, True):
        for p in range(STEPS):
            wide = (PARTS[p] - EARLY[p] if late else EARLY[p]) * LANES
            spans.append((p, starts[p] + (EARLY[p] * LANES if late else 0), wide))
    own_codes, w_own, w_far, accs = own_part(own, own_sib, dec_weight, spans)
    far, w_far = lax.optimization_barrier((xor_swap(own, "layer", 2), w_far))
    far_codes = join(far, xor_swap(far, "layer", 1))

    last = [None] * STEPS

    def exchange(data, link):
        if last[link] is not None:
            data = lax.optimization_barrier((data, last[link]))[0]
        last[link] = xor_swap(data, "lat", LINKS[link])
        return last[link]

    got = [
        exchange(decode_send(far_codes, w_far, acc, p, at), p)
        for (p, at, _), acc in zip(spans, accs)
    ]
    keeps = [
        decode_keep(own_codes, far_codes, w_own, w_far, p, starts[p], PARTS[p] * LANES)
        for p in range(STEPS)
    ]
    first, *keeps = lax.optimization_barrier((got[STEPS], *keeps))
    got[STEPS] = first
    kept, out = {}, {}
    for p in range(STEPS):
        kept[p], out[p] = merge(keeps[p], got[p], got[STEPS + p])
    for i in range(1, STEPS):
        for p in range(STEPS):
            total = kept[p] + exchange(out[p], (p + i) % STEPS).astype(F32)
            m = total.shape[0] // 2
            kept[p] = total[:m] if i < STEPS - 1 else total
            out[p] = total[m:].astype(BF16)
    summed = jnp.concatenate([kept[p] for p in range(STEPS)], axis=1)
    return (summed + dec_bias).astype(BF16)[None]


def solution(mesh):
    return jax.shard_map(
        shards,
        mesh=mesh,
        in_specs=(
            P("layer", None, None),
            P("layer", None, "lat"),
            P(None, "lat"),
            P(None, "lat"),
            P("layer", None, "lat", None),
            P("layer", None),
            P(),
            P(),
            P(),
            P(),
        ),
        out_specs=P("layer", "lat", None),
        check_vma=False,
    )
```

```python
import functools

import jax
import jax.numpy as jnp
from jax import lax
from jax.experimental import pallas as pl
from jax.experimental.pallas import tpu as pltpu
from jax.sharding import PartitionSpec as P

BF16, F32 = jnp.bfloat16, jnp.float32
LINKS = (8, 1, 4, 24, 3)
STEPS = len(LINKS)
LANES, TILE = 128, 256
PARTS = (12, 13, 13, 13, 13)
EARLY = (6, 6, 6, 6, 6)
READY = 4
VMEM = pl.BlockSpec(memory_space=pltpu.VMEM)
HBM = pl.BlockSpec(memory_space=pltpu.HBM)
MIB = 1 << 20
COPIES = 4


def xor_swap(value, axis, mask):
    return lax.ppermute(value, axis, [(i, i ^ mask) for i in range(lax.axis_size(axis))])


def block_masks():
    n = 1 << STEPS
    out = []
    for j in range(n):
        m = 0
        for k in range(STEPS):
            if (j >> (STEPS - 1 - k)) & 1:
                m ^= LINKS[k]
        out.append(m)
    return out


def part_blocks(first):
    out = []
    for j in range(1 << STEPS):
        base = 0
        for i in range(STEPS):
            if (j >> (STEPS - 1 - i)) & 1:
                base |= 1 << (STEPS - 1 - (first + i) % STEPS)
        out.append(base)
    return out


def encode_kernel(
    x_hbm, w_hbm, keep_ref, send_ref, xbuf, wbuf, xsem, wsem, *, masks, rows, chunks
):
    me = lax.axis_index("lat")
    core = lax.axis_index("layer") % 2
    width = w_hbm.shape[2] // 2
    copies = []
    for k, (at, depth) in enumerate(chunks):
        ks = pl.ds(at, depth)
        mine = [pltpu.make_async_copy(w_hbm.at[0, ks], wbuf.at[ks], wsem.at[k])]
        for j, mask in enumerate(masks):
            src = pl.multiple_of(jnp.bitwise_xor(me, mask) * rows, rows)
            mine.append(
                pltpu.make_async_copy(
                    x_hbm.at[0, pl.ds(src, rows), ks],
                    xbuf.at[pl.ds(j * rows, rows), ks],
                    xsem.at[k * len(masks) + j],
                )
            )
        copies.append(mine)
    for mine in copies:
        for c in mine:
            c.start()
    half = (
        pl.ds(pl.multiple_of((1 - core) * width, width), width),
        pl.ds(pl.multiple_of(core * width, width), width),
    )
    for k, (at, depth) in enumerate(chunks):
        for c in copies[k]:
            c.wait()
        ks = pl.ds(at, depth)
        for ref, cols in zip((send_ref, keep_ref), half):
            d = jnp.dot(xbuf[:, ks], wbuf[ks, cols], preferred_element_type=F32)
            ref[...] = d if k == 0 else ref[...] + d


def encode(x, w):
    tokens, depth = x.shape[1], x.shape[2]
    width = w.shape[2] // 2
    masks = block_masks()
    rows = tokens // len(masks)
    q = depth // 4
    chunks = ((0, q), (q, 3 * q))
    half = pltpu.VMEM((tokens, width), F32)
    return pl.pallas_call(
        functools.partial(encode_kernel, masks=masks, rows=rows, chunks=chunks),
        out_shape=(half, half),
        in_specs=[HBM] * 2,
        out_specs=[VMEM] * 2,
        scratch_shapes=[
            pltpu.VMEM((tokens, depth), BF16),
            pltpu.VMEM((depth, 2 * width), BF16),
            pltpu.SemaphoreType.DMA((len(masks) * len(chunks),)),
            pltpu.SemaphoreType.DMA((len(chunks),)),
        ],
        compiler_params=pltpu.CompilerParams(vmem_limit_bytes=54 * MIB),
        cost_estimate=pl.CostEstimate(
            flops=4 * tokens * depth * width,
            bytes_accessed=2 * (tokens * depth + 2 * depth * width) + 8 * tokens * width,
            transcendentals=0,
        ),
        name="encode",
    )(x, w)


def copy_weights(dec_hbm, source, out_ref, sem, start):
    step = out_ref.shape[0] // COPIES
    for q in range(COPIES):
        at = pl.ds(q * step, step)
        c = pltpu.make_async_copy(dec_hbm.at[0, source, at], out_ref.at[at], sem.at[q])
        if start:
            c.start()
        else:
            c.wait()


def join_kernel(mine_ref, sib_ref, out_ref):
    core = lax.axis_index("layer") % 2
    hw = mine_ref.shape[1]
    out_ref[:, pl.ds(pl.multiple_of(core * hw, hw), hw)] = mine_ref[...]
    out_ref[:, pl.ds(pl.multiple_of((1 - core) * hw, hw), hw)] = sib_ref[...]


def assemble_kernel(own_ref, own_sib_ref, far_ref, far_sib_ref, out_ref):
    group = lax.axis_index("layer")
    source, core = group // 2, group % 2
    hw = own_ref.shape[1]
    for ref, s, c in (
        (own_ref, source, core),
        (own_sib_ref, source, 1 - core),
        (far_ref, 1 - source, core),
        (far_sib_ref, 1 - source, 1 - core),
    ):
        out_ref[:, pl.ds(pl.multiple_of((s * 2 + c) * hw, hw), hw)] = ref[...]


def assemble(*pieces):
    n, hw = pieces[0].shape
    return pl.pallas_call(
        assemble_kernel,
        out_shape=pltpu.VMEM((n, 4 * hw), BF16),
        in_specs=[VMEM] * 4,
        out_specs=VMEM,
        compiler_params=pltpu.CompilerParams(vmem_limit_bytes=8 * MIB),
        name="assemble",
    )(*pieces)


def gather_rows(codes_ref, lhs, blocks, cols=slice(None)):
    rows = lhs.shape[0] // len(blocks)
    for j, b in enumerate(blocks):
        lhs[pl.ds(j * rows, rows), :] = codes_ref[pl.ds(b * rows, rows), cols]


def over_tiles(begin, end, body):
    whole = (end - begin) // TILE

    @pl.loop(0, whole)
    def _(t):
        body(pl.multiple_of(begin + t * TILE, LANES), TILE)

    if begin + whole * TILE < end:
        body(begin + whole * TILE, end - begin - whole * TILE)


def product(lhs, w_ref, at, n):
    cols = pl.ds(pl.multiple_of(at, LANES), n)
    w = w_ref[:, cols] if len(w_ref.shape) == 2 else w_ref[:, :, cols].reshape(lhs.shape[1], n)
    return jnp.dot(lhs[...], w, preferred_element_type=F32)


def own_kernel(mine_ref, sib_ref, dec_hbm, *refs, spans):
    w_ref, *accs = refs[: 1 + len(spans)]
    codes, lhs, own_sem, far_sem = refs[1 + len(spans) :]
    source = lax.axis_index("layer") // 2
    own, far = w_ref.at[source], w_ref.at[1 - source]
    copy_weights(dec_hbm, source, own, own_sem, True)
    copy_weights(dec_hbm, 1 - source, far, far_sem, True)
    join_kernel(mine_ref, sib_ref, codes)
    copy_weights(dec_hbm, source, own, own_sem, False)
    for (part, at, wide), acc in zip(spans, accs):
        gather_rows(codes, lhs, send_blocks(part))

        def body(c, n):
            acc[:, pl.ds(c, n)] = product(lhs, own, at + c, n)

        over_tiles(0, wide, body)
    copy_weights(dec_hbm, 1 - source, far, far_sem, False)


def own_part(mine, sib, dec, spans):
    tokens, hw = mine.shape
    _, sources, depth, wide = dec.shape
    n = tokens // 2
    weights, *accs = pl.pallas_call(
        functools.partial(own_kernel, spans=spans),
        out_shape=[pltpu.VMEM((sources, depth, wide), BF16)]
        + [pltpu.VMEM((n, span[2]), F32) for span in spans],
        in_specs=[VMEM, VMEM, HBM],
        out_specs=[VMEM] * (1 + len(spans)),
        scratch_shapes=[pltpu.VMEM((tokens, depth), BF16), pltpu.VMEM((n, depth), BF16)]
        + [pltpu.SemaphoreType.DMA((COPIES,))] * 2,
        compiler_params=pltpu.CompilerParams(vmem_limit_bytes=14 * MIB),
        cost_estimate=pl.CostEstimate(
            flops=n * depth * wide, bytes_accessed=8 * depth * wide, transcendentals=0
        ),
        name="own",
    )(mine, sib, dec)
    return weights, accs


def send_blocks(part):
    blocks = part_blocks(part)
    return blocks[len(blocks) // 2 :]


def keep_blocks(part):
    blocks = part_blocks(part)
    return blocks[: len(blocks) // 2]


def call_tiny(kernel, out_shape, scratch, name, *args):
    many = isinstance(out_shape, tuple)
    return pl.pallas_call(
        kernel,
        out_shape=out_shape,
        in_specs=[VMEM] * len(args),
        out_specs=[VMEM] * len(out_shape) if many else VMEM,
        scratch_shapes=scratch,
        compiler_params=pltpu.CompilerParams(vmem_limit_bytes=8 * MIB),
        cost_estimate=pl.CostEstimate(flops=1000, bytes_accessed=1000, transcendentals=0),
        name=name,
    )(*args)


def send_early_kernel(codes_ref, w_ref, acc_ref, send_ref, lhs, *, blocks, at):
    other = 1 - lax.axis_index("layer") // 2
    depth = lhs.shape[1]
    gather_rows(codes_ref, lhs, blocks, pl.ds(pl.multiple_of(other * depth, depth), depth))

    def body(c, n):
        cols = pl.ds(c, n)
        total = acc_ref[:, cols] + product(lhs, w_ref.at[other], at + c, n)
        send_ref[:, cols] = total.astype(BF16)

    over_tiles(0, send_ref.shape[1], body)


def send_early(codes, w, acc, part, at):
    n, wide = acc.shape
    return call_tiny(
        functools.partial(send_early_kernel, blocks=send_blocks(part), at=at),
        jax.ShapeDtypeStruct((n, wide), BF16),
        [pltpu.VMEM((n, codes.shape[1] // 2), BF16)],
        f"early{part}",
        codes,
        w,
        acc,
    )


def rows_kernel(codes_ref, w_ref, out_ref, lhs, *, blocks, at):
    gather_rows(codes_ref, lhs, blocks)

    def body(c, n):
        out_ref[:, pl.ds(c, n)] = product(lhs, w_ref, at + c, n).astype(out_ref.dtype)

    over_tiles(0, out_ref.shape[1], body)


def decode_rows(codes, w, blocks, at, wide, dtype, name):
    tokens, depth = codes.shape
    n = tokens // 2
    return call_tiny(
        functools.partial(rows_kernel, blocks=blocks, at=at),
        jax.ShapeDtypeStruct((n, wide), dtype),
        [pltpu.VMEM((n, depth), BF16)],
        name,
        codes,
        w,
    )


def merge_kernel(keep_ref, early_ref, late_ref, new_ref, send_ref):
    m = new_ref.shape[0]
    split = early_ref.shape[1]
    for got, cols in ((early_ref, pl.ds(0, split)), (late_ref, pl.ds(split, late_ref.shape[1]))):
        new_ref[:, cols] = keep_ref[:m, cols] + got[:m, :].astype(F32)
        send_ref[:, cols] = (keep_ref[m:, cols] + got[m:, :].astype(F32)).astype(BF16)


def merge(keep, early, late):
    n, wide = keep.shape
    return pl.pallas_call(
        merge_kernel,
        out_shape=(
            jax.ShapeDtypeStruct((n // 2, wide), F32),
            jax.ShapeDtypeStruct((n // 2, wide), BF16),
        ),
        in_specs=[VMEM] * 3,
        out_specs=[VMEM] * 2,
        compiler_params=pltpu.CompilerParams(vmem_limit_bytes=8 * MIB),
        cost_estimate=pl.CostEstimate(flops=1000, bytes_accessed=1000, transcendentals=0),
        name="merge",
    )(keep, early, late)


def shards(
    resid_halves,
    enc_weight,
    enc_bias,
    jump_threshold,
    dec_weight,
    dec_bias,
    clamp_rows,
    clamp_feats,
    clamp_slots,
    clamp_values,
):
    group = lax.axis_index("layer")
    me = lax.axis_index("lat")
    source, core = group // 2, group % 2
    tokens = resid_halves.shape[1]
    width = enc_weight.shape[2]
    hw = width // 2
    masks = jnp.array(block_masks(), jnp.int32)
    rows = tokens // masks.shape[0]

    keep, send = encode(resid_halves, enc_weight)
    recv = xor_swap(send, "layer", 1)

    row_token = (
        jnp.bitwise_xor(masks, me)[:, None] * rows + jnp.arange(rows, dtype=jnp.int32)[None, :]
    ).reshape(tokens)
    my_rows = lax.dynamic_index_in_dim(clamp_rows, source, 0, keepdims=False)
    my_pick = lax.dynamic_index_in_dim(
        clamp_feats * clamp_values.shape[0] + clamp_slots, source, 0, keepdims=False
    )
    row_hot = (my_rows[:, None] == row_token[None, :]).astype(F32)
    pick = jnp.dot(my_pick.astype(F32), row_hot, precision=lax.Precision.HIGHEST).astype(jnp.int32)
    feat, slot = pick // clamp_values.shape[0], pick % clamp_values.shape[0]
    slot_hot = slot[:, None] == jnp.arange(clamp_values.shape[0], dtype=jnp.int32)[None, :]
    value = jnp.sum(jnp.where(slot_hot, clamp_values[None, :], 0.0), axis=1)
    first = core * hw
    column = feat - me * width - first

    my_bias = lax.dynamic_slice(enc_bias, (source, first), (1, hw))
    my_thresh = lax.dynamic_slice(jump_threshold, (source, first), (1, hw))
    pre = keep + recv + my_bias
    ramp = jnp.clip((pre - my_thresh) / 0.25 + 1.0, 0.0, 1.0)
    hit = column[:, None] == jnp.arange(hw, dtype=jnp.int32)[None, :]
    own = jnp.where(hit, value[:, None], pre * ramp).astype(BF16)

    own_sib = xor_swap(own, "layer", 1)

    starts = [sum(PARTS[:p]) * LANES for p in range(STEPS)]
    spans = [(p, starts[p], EARLY[p] * LANES) for p in range(STEPS)]
    weights, accs = own_part(own, own_sib, dec_weight, spans)
    far, weights = lax.optimization_barrier((xor_swap(own, "layer", 2), weights))
    codes = assemble(own, own_sib, far, xor_swap(far, "layer", 1))

    last = [None] * STEPS

    def exchange(data, link):
        if last[link] is not None:
            data = lax.optimization_barrier((data, last[link]))[0]
        last[link] = xor_swap(data, "lat", LINKS[link])
        return last[link]

    early = [
        exchange(send_early(codes, weights, acc, p, at), p) for (p, at, _), acc in zip(spans, accs)
    ]
    sends = [
        decode_rows(codes, weights, send_blocks(p), at + wide, PARTS[p] * LANES - wide, BF16, f"late{p}")
        for p, at, wide in spans
    ]
    sends[:READY] = lax.optimization_barrier(tuple(sends[:READY]))
    late = [exchange(sends[p], p) for p in range(STEPS)]
    keeps = [
        decode_rows(codes, weights, keep_blocks(p), starts[p], PARTS[p] * LANES, F32, f"keep{p}")
        for p in range(STEPS)
    ]
    late[0], *keeps[:READY] = lax.optimization_barrier((late[0], *keeps[:READY]))
    kept, out = {}, {}
    for p in range(STEPS):
        kept[p], out[p] = merge(keeps[p], early[p], late[p])
    for i in range(1, STEPS):
        for p in range(STEPS):
            total = kept[p] + exchange(out[p], (p + i) % STEPS).astype(F32)
            m = total.shape[0] // 2
            kept[p] = total[:m] if i < STEPS - 1 else total
            out[p] = total[m:].astype(BF16)
    summed = jnp.concatenate([kept[p] for p in range(STEPS)], axis=1)
    return (summed + dec_bias).astype(BF16)[None]


def solution(mesh):
    return jax.shard_map(
        shards,
        mesh=mesh,
        in_specs=(
            P("layer", None, None),
            P("layer", None, "lat"),
            P(None, "lat"),
            P(None, "lat"),
            P("layer", None, "lat", None),
            P("layer", None),
            P(),
            P(),
            P(),
            P(),
        ),
        out_specs=P("layer", "lat", None),
        check_vma=False,
    )
```

```python
import functools

import jax
import jax.numpy as jnp
from jax import lax
from jax.experimental import pallas as pl
from jax.experimental.pallas import tpu as pltpu
from jax.sharding import PartitionSpec as P

BF16, F32 = jnp.bfloat16, jnp.float32
LINKS = (8, 1, 4, 24, 3)
STEPS = len(LINKS)
LANES, TILE = 128, 256
PARTS = (12, 13, 13, 13, 13)
AHEAD = 4
READY = 5
VMEM = pl.BlockSpec(memory_space=pltpu.VMEM)
HBM = pl.BlockSpec(memory_space=pltpu.HBM)
MIB = 1 << 20
COPIES = 4


def xor_swap(value, axis, mask):
    return lax.ppermute(value, axis, [(i, i ^ mask) for i in range(lax.axis_size(axis))])


def block_masks():
    n = 1 << STEPS
    out = []
    for j in range(n):
        m = 0
        for k in range(STEPS):
            if (j >> (STEPS - 1 - k)) & 1:
                m ^= LINKS[k]
        out.append(m)
    return out


def part_blocks(first):
    out = []
    for j in range(1 << STEPS):
        base = 0
        for i in range(STEPS):
            if (j >> (STEPS - 1 - i)) & 1:
                base |= 1 << (STEPS - 1 - (first + i) % STEPS)
        out.append(base)
    return out


def encode_kernel(
    x_hbm, w_hbm, keep_ref, send_ref, xbuf, wbuf, xsem, wsem, *, masks, rows, chunks
):
    me = lax.axis_index("lat")
    core = lax.axis_index("layer") % 2
    width = w_hbm.shape[2] // 2
    copies = []
    for k, (at, depth) in enumerate(chunks):
        ks = pl.ds(at, depth)
        mine = [pltpu.make_async_copy(w_hbm.at[0, ks], wbuf.at[ks], wsem.at[k])]
        for j, mask in enumerate(masks):
            src = pl.multiple_of(jnp.bitwise_xor(me, mask) * rows, rows)
            mine.append(
                pltpu.make_async_copy(
                    x_hbm.at[0, pl.ds(src, rows), ks],
                    xbuf.at[pl.ds(j * rows, rows), ks],
                    xsem.at[k * len(masks) + j],
                )
            )
        copies.append(mine)
    for mine in copies:
        for c in mine:
            c.start()
    half = (
        pl.ds(pl.multiple_of((1 - core) * width, width), width),
        pl.ds(pl.multiple_of(core * width, width), width),
    )
    for k, (at, depth) in enumerate(chunks):
        for c in copies[k]:
            c.wait()
        ks = pl.ds(at, depth)
        for ref, cols in zip((send_ref, keep_ref), half):
            d = jnp.dot(xbuf[:, ks], wbuf[ks, cols], preferred_element_type=F32)
            ref[...] = d if k == 0 else ref[...] + d


def encode(x, w):
    tokens, depth = x.shape[1], x.shape[2]
    width = w.shape[2] // 2
    masks = block_masks()
    rows = tokens // len(masks)
    q = depth // 4
    chunks = ((0, q), (q, 3 * q))
    half = pltpu.VMEM((tokens, width), F32)
    return pl.pallas_call(
        functools.partial(encode_kernel, masks=masks, rows=rows, chunks=chunks),
        out_shape=(half, half),
        in_specs=[HBM] * 2,
        out_specs=[VMEM] * 2,
        scratch_shapes=[
            pltpu.VMEM((tokens, depth), BF16),
            pltpu.VMEM((depth, 2 * width), BF16),
            pltpu.SemaphoreType.DMA((len(masks) * len(chunks),)),
            pltpu.SemaphoreType.DMA((len(chunks),)),
        ],
        compiler_params=pltpu.CompilerParams(vmem_limit_bytes=54 * MIB),
        cost_estimate=pl.CostEstimate(
            flops=4 * tokens * depth * width,
            bytes_accessed=2 * (tokens * depth + 2 * depth * width) + 8 * tokens * width,
            transcendentals=0,
        ),
        name="encode",
    )(x, w)


def copy_weights(dec_hbm, source, out_ref, sem, start):
    step = out_ref.shape[0] // COPIES
    for q in range(COPIES):
        at = pl.ds(q * step, step)
        c = pltpu.make_async_copy(dec_hbm.at[0, source, at], out_ref.at[at], sem.at[q])
        if start:
            c.start()
        else:
            c.wait()


def join_kernel(mine_ref, sib_ref, out_ref):
    core = lax.axis_index("layer") % 2
    hw = mine_ref.shape[1]
    out_ref[:, pl.ds(pl.multiple_of(core * hw, hw), hw)] = mine_ref[...]
    out_ref[:, pl.ds(pl.multiple_of((1 - core) * hw, hw), hw)] = sib_ref[...]


def assemble_kernel(own_ref, own_sib_ref, far_ref, far_sib_ref, out_ref):
    group = lax.axis_index("layer")
    source, core = group // 2, group % 2
    hw = own_ref.shape[1]
    for ref, s, c in (
        (own_ref, source, core),
        (own_sib_ref, source, 1 - core),
        (far_ref, 1 - source, core),
        (far_sib_ref, 1 - source, 1 - core),
    ):
        out_ref[:, pl.ds(pl.multiple_of((s * 2 + c) * hw, hw), hw)] = ref[...]


def assemble(*pieces):
    n, hw = pieces[0].shape
    return pl.pallas_call(
        assemble_kernel,
        out_shape=pltpu.VMEM((n, 4 * hw), BF16),
        in_specs=[VMEM] * 4,
        out_specs=VMEM,
        compiler_params=pltpu.CompilerParams(vmem_limit_bytes=8 * MIB),
        name="assemble",
    )(*pieces)


def gather_rows(codes_ref, lhs, blocks, cols=slice(None)):
    rows = lhs.shape[0] // len(blocks)
    for j, b in enumerate(blocks):
        lhs[pl.ds(j * rows, rows), :] = codes_ref[pl.ds(b * rows, rows), cols]


def over_tiles(begin, end, body):
    whole = (end - begin) // TILE

    @pl.loop(0, whole)
    def _(t):
        body(pl.multiple_of(begin + t * TILE, LANES), TILE)

    if begin + whole * TILE < end:
        body(begin + whole * TILE, end - begin - whole * TILE)


def product(lhs, w_ref, at, n):
    cols = pl.ds(pl.multiple_of(at, LANES), n)
    w = w_ref[:, cols] if len(w_ref.shape) == 2 else w_ref[:, :, cols].reshape(lhs.shape[1], n)
    return jnp.dot(lhs[...], w, preferred_element_type=F32)


def own_kernel(mine_ref, sib_ref, dec_hbm, *refs, spans):
    w_ref, *accs = refs[: 1 + len(spans)]
    codes, lhs, own_sem, far_sem = refs[1 + len(spans) :]
    source = lax.axis_index("layer") // 2
    own, far = w_ref.at[source], w_ref.at[1 - source]
    copy_weights(dec_hbm, source, own, own_sem, True)
    copy_weights(dec_hbm, 1 - source, far, far_sem, True)
    join_kernel(mine_ref, sib_ref, codes)
    copy_weights(dec_hbm, source, own, own_sem, False)
    for (part, at, wide), acc in zip(spans, accs):
        gather_rows(codes, lhs, send_blocks(part))

        def body(c, n):
            acc[:, pl.ds(c, n)] = product(lhs, own, at + c, n)

        over_tiles(0, wide, body)
    copy_weights(dec_hbm, 1 - source, far, far_sem, False)


def own_rest_kernel(mine_ref, sib_ref, w_ref, acc, codes, lhs, *, part, at):
    source = lax.axis_index("layer") // 2
    join_kernel(mine_ref, sib_ref, codes)
    gather_rows(codes, lhs, send_blocks(part))

    def body(c, n):
        acc[:, pl.ds(c, n)] = product(lhs, w_ref.at[source], at + c, n)

    over_tiles(0, acc.shape[1], body)


def own_rest(mine, sib, w, part, at, wide):
    tokens, hw = mine.shape
    n = tokens // 2
    return call_tiny(
        functools.partial(own_rest_kernel, part=part, at=at),
        jax.ShapeDtypeStruct((n, wide), F32),
        [pltpu.VMEM((tokens, 2 * hw), BF16), pltpu.VMEM((n, 2 * hw), BF16)],
        "rest",
        mine,
        sib,
        w,
    )


def own_part(mine, sib, dec, spans):
    tokens, hw = mine.shape
    _, sources, depth, wide = dec.shape
    n = tokens // 2
    weights, *accs = pl.pallas_call(
        functools.partial(own_kernel, spans=spans),
        out_shape=[pltpu.VMEM((sources, depth, wide), BF16)]
        + [pltpu.VMEM((n, span[2]), F32) for span in spans],
        in_specs=[VMEM, VMEM, HBM],
        out_specs=[VMEM] * (1 + len(spans)),
        scratch_shapes=[pltpu.VMEM((tokens, depth), BF16), pltpu.VMEM((n, depth), BF16)]
        + [pltpu.SemaphoreType.DMA((COPIES,))] * 2,
        compiler_params=pltpu.CompilerParams(vmem_limit_bytes=14 * MIB),
        cost_estimate=pl.CostEstimate(
            flops=n * depth * wide, bytes_accessed=8 * depth * wide, transcendentals=0
        ),
        name="own",
    )(mine, sib, dec)
    return weights, accs


def send_blocks(part):
    blocks = part_blocks(part)
    return blocks[len(blocks) // 2 :]


def keep_blocks(part):
    blocks = part_blocks(part)
    return blocks[: len(blocks) // 2]


def call_tiny(kernel, out_shape, scratch, name, *args):
    many = isinstance(out_shape, tuple)
    return pl.pallas_call(
        kernel,
        out_shape=out_shape,
        in_specs=[VMEM] * len(args),
        out_specs=[VMEM] * len(out_shape) if many else VMEM,
        scratch_shapes=scratch,
        compiler_params=pltpu.CompilerParams(vmem_limit_bytes=8 * MIB),
        cost_estimate=pl.CostEstimate(flops=1000, bytes_accessed=1000, transcendentals=0),
        name=name,
    )(*args)


def decode_send_kernel(codes_ref, w_ref, acc_ref, send_ref, lhs, *, blocks, at):
    other = 1 - lax.axis_index("layer") // 2
    depth = lhs.shape[1]
    gather_rows(codes_ref, lhs, blocks, pl.ds(pl.multiple_of(other * depth, depth), depth))

    def body(c, n):
        cols = pl.ds(c, n)
        total = acc_ref[:, cols] + product(lhs, w_ref.at[other], at + c, n)
        send_ref[:, cols] = total.astype(BF16)

    over_tiles(0, send_ref.shape[1], body)


def decode_send(codes, w, acc, part, at):
    n, wide = acc.shape
    return call_tiny(
        functools.partial(decode_send_kernel, blocks=send_blocks(part), at=at),
        jax.ShapeDtypeStruct((n, wide), BF16),
        [pltpu.VMEM((n, codes.shape[1] // 2), BF16)],
        f"send{part}",
        codes,
        w,
        acc,
    )


def rows_kernel(codes_ref, w_ref, out_ref, lhs, *, blocks, at):
    gather_rows(codes_ref, lhs, blocks)

    def body(c, n):
        out_ref[:, pl.ds(c, n)] = product(lhs, w_ref, at + c, n).astype(out_ref.dtype)

    over_tiles(0, out_ref.shape[1], body)


def decode_rows(codes, w, blocks, at, wide, dtype, name):
    tokens, depth = codes.shape
    n = tokens // 2
    return call_tiny(
        functools.partial(rows_kernel, blocks=blocks, at=at),
        jax.ShapeDtypeStruct((n, wide), dtype),
        [pltpu.VMEM((n, depth), BF16)],
        name,
        codes,
        w,
    )


def merge_kernel(keep_ref, got_ref, new_ref, send_ref):
    m = new_ref.shape[0]
    new_ref[...] = keep_ref[:m, :] + got_ref[:m, :].astype(F32)
    send_ref[...] = (keep_ref[m:, :] + got_ref[m:, :].astype(F32)).astype(BF16)


def merge(keep, got):
    n, wide = keep.shape
    out = tuple(jax.ShapeDtypeStruct((n // 2, wide), dtype) for dtype in (F32, BF16))
    return call_tiny(merge_kernel, out, [], "merge", keep, got)


def shards(
    resid_halves,
    enc_weight,
    enc_bias,
    jump_threshold,
    dec_weight,
    dec_bias,
    clamp_rows,
    clamp_feats,
    clamp_slots,
    clamp_values,
):
    group = lax.axis_index("layer")
    me = lax.axis_index("lat")
    source, core = group // 2, group % 2
    tokens = resid_halves.shape[1]
    width = enc_weight.shape[2]
    hw = width // 2
    masks = jnp.array(block_masks(), jnp.int32)
    rows = tokens // masks.shape[0]

    keep, send = encode(resid_halves, enc_weight)
    recv = xor_swap(send, "layer", 1)

    row_token = (
        jnp.bitwise_xor(masks, me)[:, None] * rows + jnp.arange(rows, dtype=jnp.int32)[None, :]
    ).reshape(tokens)
    my_rows = lax.dynamic_index_in_dim(clamp_rows, source, 0, keepdims=False)
    my_pick = lax.dynamic_index_in_dim(
        clamp_feats * clamp_values.shape[0] + clamp_slots, source, 0, keepdims=False
    )
    row_hot = (my_rows[:, None] == row_token[None, :]).astype(F32)
    pick = jnp.dot(my_pick.astype(F32), row_hot, precision=lax.Precision.HIGHEST).astype(jnp.int32)
    feat, slot = pick // clamp_values.shape[0], pick % clamp_values.shape[0]
    slot_hot = slot[:, None] == jnp.arange(clamp_values.shape[0], dtype=jnp.int32)[None, :]
    value = jnp.sum(jnp.where(slot_hot, clamp_values[None, :], 0.0), axis=1)
    first = core * hw
    column = feat - me * width - first

    my_bias = lax.dynamic_slice(enc_bias, (source, first), (1, hw))
    my_thresh = lax.dynamic_slice(jump_threshold, (source, first), (1, hw))
    pre = keep + recv + my_bias
    ramp = jnp.clip((pre - my_thresh) / 0.25 + 1.0, 0.0, 1.0)
    hit = column[:, None] == jnp.arange(hw, dtype=jnp.int32)[None, :]
    own = jnp.where(hit, value[:, None], pre * ramp).astype(BF16)

    own_sib = xor_swap(own, "layer", 1)

    starts = [sum(PARTS[:p]) * LANES for p in range(STEPS)]
    spans = [(p, starts[p], PARTS[p] * LANES) for p in range(STEPS)]
    weights, accs = own_part(own, own_sib, dec_weight, spans[:AHEAD])
    far, weights = lax.optimization_barrier((xor_swap(own, "layer", 2), weights))
    far_sib = xor_swap(far, "layer", 1)
    accs += [own_rest(own, own_sib, weights, *span) for span in spans[AHEAD:]]
    far_sib, *accs = lax.optimization_barrier((far_sib, *accs))
    codes = assemble(own, own_sib, far, far_sib)

    last = [None] * STEPS

    def exchange(data, link):
        if last[link] is not None:
            data = lax.optimization_barrier((data, last[link]))[0]
        last[link] = xor_swap(data, "lat", LINKS[link])
        return last[link]

    got = [
        exchange(decode_send(codes, weights, acc, p, at), p) for (p, at, _), acc in zip(spans, accs)
    ]
    keeps = [
        decode_rows(codes, weights, keep_blocks(p), at, wide, F32, f"keep{p}") for p, at, wide in spans
    ]
    got[0], *keeps[:READY] = lax.optimization_barrier((got[0], *keeps[:READY]))
    kept, out = {}, {}
    for p in range(STEPS):
        kept[p], out[p] = merge(keeps[p], got[p])
    for i in range(1, STEPS):
        for p in range(STEPS):
            total = kept[p] + exchange(out[p], (p + i) % STEPS).astype(F32)
            m = total.shape[0] // 2
            kept[p] = total[:m] if i < STEPS - 1 else total
            out[p] = total[m:].astype(BF16)
    summed = jnp.concatenate([kept[p] for p in range(STEPS)], axis=1)
    return (summed + dec_bias).astype(BF16)[None]


def solution(mesh):
    return jax.shard_map(
        shards,
        mesh=mesh,
        in_specs=(
            P("layer", None, None),
            P("layer", None, "lat"),
            P(None, "lat"),
            P(None, "lat"),
            P("layer", None, "lat", None),
            P("layer", None),
            P(),
            P(),
            P(),
            P(),
        ),
        out_specs=P("layer", "lat", None),
        check_vma=False,
    )
```

```python
import functools

import jax
import jax.numpy as jnp
from jax import lax
from jax.experimental import pallas as pl
from jax.experimental.pallas import tpu as pltpu
from jax.sharding import PartitionSpec as P

BF16, F32 = jnp.bfloat16, jnp.float32
LINKS = (8, 1, 4, 24, 3)
STEPS = len(LINKS)
LANES, TILE = 128, 256
PARTS = (12, 13, 13, 13, 13)
EARLY = (6, 6, 6, 6, 6)
READY = 3
KEPT = 3
FIRST = 0
VMEM = pl.BlockSpec(memory_space=pltpu.VMEM)
HBM = pl.BlockSpec(memory_space=pltpu.HBM)
MIB = 1 << 20
COPIES = 4


def xor_swap(value, axis, mask):
    return lax.ppermute(value, axis, [(i, i ^ mask) for i in range(lax.axis_size(axis))])


def block_masks():
    n = 1 << STEPS
    out = []
    for j in range(n):
        m = 0
        for k in range(STEPS):
            if (j >> (STEPS - 1 - k)) & 1:
                m ^= LINKS[k]
        out.append(m)
    return out


def part_blocks(first):
    out = []
    for j in range(1 << STEPS):
        base = 0
        for i in range(STEPS):
            if (j >> (STEPS - 1 - i)) & 1:
                base |= 1 << (STEPS - 1 - (first + i) % STEPS)
        out.append(base)
    return out


def encode_kernel(
    x_hbm, w_hbm, keep_ref, send_ref, xbuf, wbuf, xsem, wsem, *, masks, rows, chunks
):
    me = lax.axis_index("lat")
    core = lax.axis_index("layer") % 2
    width = w_hbm.shape[2] // 2
    copies = []
    for k, (at, depth) in enumerate(chunks):
        ks = pl.ds(at, depth)
        mine = [pltpu.make_async_copy(w_hbm.at[0, ks], wbuf.at[ks], wsem.at[k])]
        for j, mask in enumerate(masks):
            src = pl.multiple_of(jnp.bitwise_xor(me, mask) * rows, rows)
            mine.append(
                pltpu.make_async_copy(
                    x_hbm.at[0, pl.ds(src, rows), ks],
                    xbuf.at[pl.ds(j * rows, rows), ks],
                    xsem.at[k * len(masks) + j],
                )
            )
        copies.append(mine)
    for mine in copies:
        for c in mine:
            c.start()
    half = (
        pl.ds(pl.multiple_of((1 - core) * width, width), width),
        pl.ds(pl.multiple_of(core * width, width), width),
    )
    for k, (at, depth) in enumerate(chunks):
        for c in copies[k]:
            c.wait()
        ks = pl.ds(at, depth)
        for ref, cols in zip((send_ref, keep_ref), half):
            d = jnp.dot(xbuf[:, ks], wbuf[ks, cols], preferred_element_type=F32)
            ref[...] = d if k == 0 else ref[...] + d


def encode(x, w):
    tokens, depth = x.shape[1], x.shape[2]
    width = w.shape[2] // 2
    masks = block_masks()
    rows = tokens // len(masks)
    q = depth // 4
    chunks = ((0, q), (q, 3 * q))
    half = pltpu.VMEM((tokens, width), F32)
    return pl.pallas_call(
        functools.partial(encode_kernel, masks=masks, rows=rows, chunks=chunks),
        out_shape=(half, half),
        in_specs=[HBM] * 2,
        out_specs=[VMEM] * 2,
        scratch_shapes=[
            pltpu.VMEM((tokens, depth), BF16),
            pltpu.VMEM((depth, 2 * width), BF16),
            pltpu.SemaphoreType.DMA((len(masks) * len(chunks),)),
            pltpu.SemaphoreType.DMA((len(chunks),)),
        ],
        compiler_params=pltpu.CompilerParams(vmem_limit_bytes=54 * MIB),
        cost_estimate=pl.CostEstimate(
            flops=4 * tokens * depth * width,
            bytes_accessed=2 * (tokens * depth + 2 * depth * width) + 8 * tokens * width,
            transcendentals=0,
        ),
        name="encode",
    )(x, w)


def copy_weights(dec_hbm, source, out_ref, sem, start):
    step = out_ref.shape[0] // COPIES
    for q in range(COPIES):
        at = pl.ds(q * step, step)
        c = pltpu.make_async_copy(dec_hbm.at[0, source, at], out_ref.at[at], sem.at[q])
        if start:
            c.start()
        else:
            c.wait()


def join_kernel(mine_ref, sib_ref, out_ref):
    core = lax.axis_index("layer") % 2
    hw = mine_ref.shape[1]
    out_ref[:, pl.ds(pl.multiple_of(core * hw, hw), hw)] = mine_ref[...]
    out_ref[:, pl.ds(pl.multiple_of((1 - core) * hw, hw), hw)] = sib_ref[...]


def assemble_kernel(own_ref, own_sib_ref, far_ref, far_sib_ref, out_ref):
    group = lax.axis_index("layer")
    source, core = group // 2, group % 2
    hw = own_ref.shape[1]
    for ref, s, c in (
        (own_ref, source, core),
        (own_sib_ref, source, 1 - core),
        (far_ref, 1 - source, core),
        (far_sib_ref, 1 - source, 1 - core),
    ):
        out_ref[:, pl.ds(pl.multiple_of((s * 2 + c) * hw, hw), hw)] = ref[...]


def assemble(*pieces):
    n, hw = pieces[0].shape
    return pl.pallas_call(
        assemble_kernel,
        out_shape=pltpu.VMEM((n, 4 * hw), BF16),
        in_specs=[VMEM] * 4,
        out_specs=VMEM,
        compiler_params=pltpu.CompilerParams(vmem_limit_bytes=8 * MIB),
        name="assemble",
    )(*pieces)


def gather_rows(codes_ref, lhs, blocks, cols=slice(None)):
    rows = lhs.shape[0] // len(blocks)
    for j, b in enumerate(blocks):
        lhs[pl.ds(j * rows, rows), :] = codes_ref[pl.ds(b * rows, rows), cols]


def over_tiles(begin, end, body):
    whole = (end - begin) // TILE

    @pl.loop(0, whole)
    def _(t):
        body(pl.multiple_of(begin + t * TILE, LANES), TILE)

    if begin + whole * TILE < end:
        body(begin + whole * TILE, end - begin - whole * TILE)


def product(lhs, w_ref, at, n):
    cols = pl.ds(pl.multiple_of(at, LANES), n)
    w = w_ref[:, cols] if len(w_ref.shape) == 2 else w_ref[:, :, cols].reshape(lhs.shape[1], n)
    return jnp.dot(lhs[...], w, preferred_element_type=F32)


def own_kernel(mine_ref, sib_ref, dec_hbm, *refs, spans):
    w_ref, *accs = refs[: 1 + len(spans)]
    codes, lhs, own_sem, far_sem = refs[1 + len(spans) :]
    source = lax.axis_index("layer") // 2
    own, far = w_ref.at[source], w_ref.at[1 - source]
    copy_weights(dec_hbm, source, own, own_sem, True)
    copy_weights(dec_hbm, 1 - source, far, far_sem, True)
    join_kernel(mine_ref, sib_ref, codes)
    copy_weights(dec_hbm, source, own, own_sem, False)
    for (part, at, wide), acc in zip(spans, accs):
        gather_rows(codes, lhs, send_blocks(part))

        def body(c, n):
            acc[:, pl.ds(c, n)] = product(lhs, own, at + c, n)

        over_tiles(0, wide, body)
    copy_weights(dec_hbm, 1 - source, far, far_sem, False)


def own_part(mine, sib, dec, spans):
    tokens, hw = mine.shape
    _, sources, depth, wide = dec.shape
    n = tokens // 2
    weights, *accs = pl.pallas_call(
        functools.partial(own_kernel, spans=spans),
        out_shape=[pltpu.VMEM((sources, depth, wide), BF16)]
        + [pltpu.VMEM((n, span[2]), F32) for span in spans],
        in_specs=[VMEM, VMEM, HBM],
        out_specs=[VMEM] * (1 + len(spans)),
        scratch_shapes=[pltpu.VMEM((tokens, depth), BF16), pltpu.VMEM((n, depth), BF16)]
        + [pltpu.SemaphoreType.DMA((COPIES,))] * 2,
        compiler_params=pltpu.CompilerParams(vmem_limit_bytes=14 * MIB),
        cost_estimate=pl.CostEstimate(
            flops=n * depth * wide, bytes_accessed=8 * depth * wide, transcendentals=0
        ),
        name="own",
    )(mine, sib, dec)
    return weights, accs


def send_blocks(part):
    blocks = part_blocks(part)
    return blocks[len(blocks) // 2 :]


def keep_blocks(part):
    blocks = part_blocks(part)
    return blocks[: len(blocks) // 2]


def call_tiny(kernel, out_shape, scratch, name, *args):
    many = isinstance(out_shape, tuple)
    return pl.pallas_call(
        kernel,
        out_shape=out_shape,
        in_specs=[VMEM] * len(args),
        out_specs=[VMEM] * len(out_shape) if many else VMEM,
        scratch_shapes=scratch,
        compiler_params=pltpu.CompilerParams(vmem_limit_bytes=8 * MIB),
        cost_estimate=pl.CostEstimate(flops=1000, bytes_accessed=1000, transcendentals=0),
        name=name,
    )(*args)


def send_early_kernel(codes_ref, w_ref, acc_ref, send_ref, lhs, *, blocks, at):
    other = 1 - lax.axis_index("layer") // 2
    depth = lhs.shape[1]
    gather_rows(codes_ref, lhs, blocks, pl.ds(pl.multiple_of(other * depth, depth), depth))

    def body(c, n):
        cols = pl.ds(c, n)
        total = acc_ref[:, cols] + product(lhs, w_ref.at[other], at + c, n)
        send_ref[:, cols] = total.astype(BF16)

    over_tiles(0, send_ref.shape[1], body)


def send_early(codes, w, acc, part, at):
    n, wide = acc.shape
    return call_tiny(
        functools.partial(send_early_kernel, blocks=send_blocks(part), at=at),
        jax.ShapeDtypeStruct((n, wide), BF16),
        [pltpu.VMEM((n, codes.shape[1] // 2), BF16)],
        f"early{part}",
        codes,
        w,
        acc,
    )


def rows_kernel(codes_ref, w_ref, out_ref, lhs, *, blocks, at):
    gather_rows(codes_ref, lhs, blocks)

    def body(c, n):
        out_ref[:, pl.ds(c, n)] = product(lhs, w_ref, at + c, n).astype(out_ref.dtype)

    over_tiles(0, out_ref.shape[1], body)


def decode_rows(codes, w, blocks, at, wide, dtype, name):
    tokens, depth = codes.shape
    n = tokens // 2
    return call_tiny(
        functools.partial(rows_kernel, blocks=blocks, at=at),
        jax.ShapeDtypeStruct((n, wide), dtype),
        [pltpu.VMEM((n, depth), BF16)],
        name,
        codes,
        w,
    )


def merge_kernel(keep_ref, early_ref, late_ref, new_ref, send_ref):
    m = new_ref.shape[0]
    split = early_ref.shape[1]
    for got, cols in ((early_ref, pl.ds(0, split)), (late_ref, pl.ds(split, late_ref.shape[1]))):
        new_ref[:, cols] = keep_ref[:m, cols] + got[:m, :].astype(F32)
        send_ref[:, cols] = (keep_ref[m:, cols] + got[m:, :].astype(F32)).astype(BF16)


def merge(keep, early, late):
    n, wide = keep.shape
    return pl.pallas_call(
        merge_kernel,
        out_shape=(
            jax.ShapeDtypeStruct((n // 2, wide), F32),
            jax.ShapeDtypeStruct((n // 2, wide), BF16),
        ),
        in_specs=[VMEM] * 3,
        out_specs=[VMEM] * 2,
        compiler_params=pltpu.CompilerParams(vmem_limit_bytes=8 * MIB),
        cost_estimate=pl.CostEstimate(flops=1000, bytes_accessed=1000, transcendentals=0),
        name="merge",
    )(keep, early, late)


def shards(
    resid_halves,
    enc_weight,
    enc_bias,
    jump_threshold,
    dec_weight,
    dec_bias,
    clamp_rows,
    clamp_feats,
    clamp_slots,
    clamp_values,
):
    group = lax.axis_index("layer")
    me = lax.axis_index("lat")
    source, core = group // 2, group % 2
    tokens = resid_halves.shape[1]
    width = enc_weight.shape[2]
    hw = width // 2
    masks = jnp.array(block_masks(), jnp.int32)
    rows = tokens // masks.shape[0]

    keep, send = encode(resid_halves, enc_weight)
    recv = xor_swap(send, "layer", 1)

    row_token = (
        jnp.bitwise_xor(masks, me)[:, None] * rows + jnp.arange(rows, dtype=jnp.int32)[None, :]
    ).reshape(tokens)
    my_rows = lax.dynamic_index_in_dim(clamp_rows, source, 0, keepdims=False)
    my_pick = lax.dynamic_index_in_dim(
        clamp_feats * clamp_values.shape[0] + clamp_slots, source, 0, keepdims=False
    )
    row_hot = (my_rows[:, None] == row_token[None, :]).astype(F32)
    pick = jnp.dot(my_pick.astype(F32), row_hot, precision=lax.Precision.HIGHEST).astype(jnp.int32)
    feat, slot = pick // clamp_values.shape[0], pick % clamp_values.shape[0]
    slot_hot = slot[:, None] == jnp.arange(clamp_values.shape[0], dtype=jnp.int32)[None, :]
    value = jnp.sum(jnp.where(slot_hot, clamp_values[None, :], 0.0), axis=1)
    first = core * hw
    column = feat - me * width - first

    my_bias = lax.dynamic_slice(enc_bias, (source, first), (1, hw))
    my_thresh = lax.dynamic_slice(jump_threshold, (source, first), (1, hw))
    pre = keep + recv + my_bias
    ramp = jnp.clip((pre - my_thresh) / 0.25 + 1.0, 0.0, 1.0)
    hit = column[:, None] == jnp.arange(hw, dtype=jnp.int32)[None, :]
    own = jnp.where(hit, value[:, None], pre * ramp).astype(BF16)

    own_sib = xor_swap(own, "layer", 1)

    starts = [sum(PARTS[:p]) * LANES for p in range(STEPS)]
    spans = [(p, starts[p], EARLY[p] * LANES) for p in range(STEPS)]
    weights, accs = own_part(own, own_sib, dec_weight, spans)
    far, weights = lax.optimization_barrier((xor_swap(own, "layer", 2), weights))
    codes = assemble(own, own_sib, far, xor_swap(far, "layer", 1))

    last = [None] * STEPS

    def exchange(data, link):
        if last[link] is not None:
            data = lax.optimization_barrier((data, last[link]))[0]
        last[link] = xor_swap(data, "lat", LINKS[link])
        return last[link]

    early = [
        exchange(send_early(codes, weights, acc, p, at), p) for (p, at, _), acc in zip(spans, accs)
    ]
    sends = [
        decode_rows(codes, weights, send_blocks(p), at + wide, PARTS[p] * LANES - wide, BF16, f"late{p}")
        for p, at, wide in spans
    ]
    sends[:READY] = lax.optimization_barrier(tuple(sends[:READY]))
    late = [exchange(sends[p], p) for p in range(STEPS)]
    keeps = [
        decode_rows(codes, weights, keep_blocks(p), starts[p], PARTS[p] * LANES, F32, f"keep{p}")
        for p in range(STEPS)
    ]
    late[FIRST], *keeps[:KEPT] = lax.optimization_barrier((late[FIRST], *keeps[:KEPT]))
    kept, out = {}, {}
    for p in range(STEPS):
        kept[p], out[p] = merge(keeps[p], early[p], late[p])
    for i in range(1, STEPS):
        for p in range(STEPS):
            total = kept[p] + xor_swap(out[p], "lat", LINKS[(p + i) % STEPS]).astype(F32)
            m = total.shape[0] // 2
            kept[p] = total[:m] if i < STEPS - 1 else total
            out[p] = total[m:].astype(BF16)
    summed = jnp.concatenate([kept[p] for p in range(STEPS)], axis=1)
    return (summed + dec_bias).astype(BF16)[None]


def solution(mesh):
    return jax.shard_map(
        shards,
        mesh=mesh,
        in_specs=(
            P("layer", None, None),
            P("layer", None, "lat"),
            P(None, "lat"),
            P(None, "lat"),
            P("layer", None, "lat", None),
            P("layer", None),
            P(),
            P(),
            P(),
            P(),
        ),
        out_specs=P("layer", "lat", None),
        check_vma=False,
    )
```

```python
import functools

import jax
import jax.numpy as jnp
from jax import lax
from jax.experimental import pallas as pl
from jax.experimental.pallas import tpu as pltpu
from jax.sharding import PartitionSpec as P

BF16, F32 = jnp.bfloat16, jnp.float32
LINKS = (8, 1, 4, 24, 3)
STEPS = len(LINKS)
LANES, TILE = 128, 256
PARTS = (12, 13, 13, 13, 13)
EARLY = (6, 6, 6, 6, 6)
READY = 3
KEPT = 3
FIRST = 0
VMEM = pl.BlockSpec(memory_space=pltpu.VMEM)
HBM = pl.BlockSpec(memory_space=pltpu.HBM)
MIB = 1 << 20
COPIES = 4


def xor_swap(value, axis, mask):
    return lax.ppermute(value, axis, [(i, i ^ mask) for i in range(lax.axis_size(axis))])


def block_masks():
    n = 1 << STEPS
    out = []
    for j in range(n):
        m = 0
        for k in range(STEPS):
            if (j >> (STEPS - 1 - k)) & 1:
                m ^= LINKS[k]
        out.append(m)
    return out


def part_blocks(first):
    out = []
    for j in range(1 << STEPS):
        base = 0
        for i in range(STEPS):
            if (j >> (STEPS - 1 - i)) & 1:
                base |= 1 << (STEPS - 1 - (first + i) % STEPS)
        out.append(base)
    return out


def encode_kernel(
    x_hbm, w_hbm, keep_ref, send_ref, xbuf, wbuf, xsem, wsem, *, masks, rows, chunks
):
    me = lax.axis_index("lat")
    core = lax.axis_index("layer") % 2
    width = w_hbm.shape[2] // 2
    copies = []
    for k, (at, depth) in enumerate(chunks):
        ks = pl.ds(at, depth)
        mine = [pltpu.make_async_copy(w_hbm.at[0, ks], wbuf.at[ks], wsem.at[k])]
        for j, mask in enumerate(masks):
            src = pl.multiple_of(jnp.bitwise_xor(me, mask) * rows, rows)
            mine.append(
                pltpu.make_async_copy(
                    x_hbm.at[0, pl.ds(src, rows), ks],
                    xbuf.at[pl.ds(j * rows, rows), ks],
                    xsem.at[k * len(masks) + j],
                )
            )
        copies.append(mine)
    for mine in copies:
        for c in mine:
            c.start()
    half = (
        pl.ds(pl.multiple_of((1 - core) * width, width), width),
        pl.ds(pl.multiple_of(core * width, width), width),
    )
    for k, (at, depth) in enumerate(chunks):
        for c in copies[k]:
            c.wait()
        ks = pl.ds(at, depth)
        for ref, cols in zip((send_ref, keep_ref), half):
            d = jnp.dot(xbuf[:, ks], wbuf[ks, cols], preferred_element_type=F32)
            ref[...] = d if k == 0 else ref[...] + d


def encode(x, w):
    tokens, depth = x.shape[1], x.shape[2]
    width = w.shape[2] // 2
    masks = block_masks()
    rows = tokens // len(masks)
    q = depth // 4
    chunks = ((0, q), (q, 3 * q))
    half = pltpu.VMEM((tokens, width), F32)
    return pl.pallas_call(
        functools.partial(encode_kernel, masks=masks, rows=rows, chunks=chunks),
        out_shape=(half, half),
        in_specs=[HBM] * 2,
        out_specs=[VMEM] * 2,
        scratch_shapes=[
            pltpu.VMEM((tokens, depth), BF16),
            pltpu.VMEM((depth, 2 * width), BF16),
            pltpu.SemaphoreType.DMA((len(masks) * len(chunks),)),
            pltpu.SemaphoreType.DMA((len(chunks),)),
        ],
        compiler_params=pltpu.CompilerParams(vmem_limit_bytes=54 * MIB),
        cost_estimate=pl.CostEstimate(
            flops=4 * tokens * depth * width,
            bytes_accessed=2 * (tokens * depth + 2 * depth * width) + 8 * tokens * width,
            transcendentals=0,
        ),
        name="encode",
    )(x, w)


def copy_weights(dec_hbm, source, out_ref, sem, start):
    step = out_ref.shape[0] // COPIES
    for q in range(COPIES):
        at = pl.ds(q * step, step)
        c = pltpu.make_async_copy(dec_hbm.at[0, source, at], out_ref.at[at], sem.at[q])
        if start:
            c.start()
        else:
            c.wait()


def join_kernel(mine_ref, sib_ref, out_ref):
    core = lax.axis_index("layer") % 2
    hw = mine_ref.shape[1]
    out_ref[:, pl.ds(pl.multiple_of(core * hw, hw), hw)] = mine_ref[...]
    out_ref[:, pl.ds(pl.multiple_of((1 - core) * hw, hw), hw)] = sib_ref[...]


def assemble_kernel(own_ref, own_sib_ref, far_ref, far_sib_ref, out_ref):
    group = lax.axis_index("layer")
    source, core = group // 2, group % 2
    hw = own_ref.shape[1]
    for ref, s, c in (
        (own_ref, source, core),
        (own_sib_ref, source, 1 - core),
        (far_ref, 1 - source, core),
        (far_sib_ref, 1 - source, 1 - core),
    ):
        out_ref[:, pl.ds(pl.multiple_of((s * 2 + c) * hw, hw), hw)] = ref[...]


def assemble(*pieces):
    n, hw = pieces[0].shape
    return pl.pallas_call(
        assemble_kernel,
        out_shape=pltpu.VMEM((n, 4 * hw), BF16),
        in_specs=[VMEM] * 4,
        out_specs=VMEM,
        compiler_params=pltpu.CompilerParams(vmem_limit_bytes=8 * MIB),
        name="assemble",
    )(*pieces)


def gather_rows(codes_ref, lhs, blocks, cols=slice(None)):
    rows = lhs.shape[0] // len(blocks)
    for j, b in enumerate(blocks):
        lhs[pl.ds(j * rows, rows), :] = codes_ref[pl.ds(b * rows, rows), cols]


def over_tiles(begin, end, body):
    whole = (end - begin) // TILE

    @pl.loop(0, whole)
    def _(t):
        body(pl.multiple_of(begin + t * TILE, LANES), TILE)

    if begin + whole * TILE < end:
        body(begin + whole * TILE, end - begin - whole * TILE)


def product(lhs, w_ref, at, n):
    cols = pl.ds(pl.multiple_of(at, LANES), n)
    w = w_ref[:, cols] if len(w_ref.shape) == 2 else w_ref[:, :, cols].reshape(lhs.shape[1], n)
    return jnp.dot(lhs[...], w, preferred_element_type=F32)


def own_kernel(mine_ref, sib_ref, dec_hbm, *refs, spans):
    w_ref, *accs = refs[: 1 + len(spans)]
    codes, lhs, own_sem, far_sem = refs[1 + len(spans) :]
    source = lax.axis_index("layer") // 2
    own, far = w_ref.at[source], w_ref.at[1 - source]
    copy_weights(dec_hbm, source, own, own_sem, True)
    copy_weights(dec_hbm, 1 - source, far, far_sem, True)
    join_kernel(mine_ref, sib_ref, codes)
    copy_weights(dec_hbm, source, own, own_sem, False)
    for (part, at, wide), acc in zip(spans, accs):
        gather_rows(codes, lhs, send_blocks(part))

        def body(c, n):
            acc[:, pl.ds(c, n)] = product(lhs, own, at + c, n)

        over_tiles(0, wide, body)
    copy_weights(dec_hbm, 1 - source, far, far_sem, False)


def own_part(mine, sib, dec, spans):
    tokens, hw = mine.shape
    _, sources, depth, wide = dec.shape
    n = tokens // 2
    weights, *accs = pl.pallas_call(
        functools.partial(own_kernel, spans=spans),
        out_shape=[pltpu.VMEM((sources, depth, wide), BF16)]
        + [pltpu.VMEM((n, span[2]), F32) for span in spans],
        in_specs=[VMEM, VMEM, HBM],
        out_specs=[VMEM] * (1 + len(spans)),
        scratch_shapes=[pltpu.VMEM((tokens, depth), BF16), pltpu.VMEM((n, depth), BF16)]
        + [pltpu.SemaphoreType.DMA((COPIES,))] * 2,
        compiler_params=pltpu.CompilerParams(vmem_limit_bytes=14 * MIB),
        cost_estimate=pl.CostEstimate(
            flops=n * depth * wide, bytes_accessed=8 * depth * wide, transcendentals=0
        ),
        name="own",
    )(mine, sib, dec)
    return weights, accs


def send_blocks(part):
    blocks = part_blocks(part)
    return blocks[len(blocks) // 2 :]


def keep_blocks(part):
    blocks = part_blocks(part)
    return blocks[: len(blocks) // 2]


def call_tiny(kernel, out_shape, scratch, name, *args):
    many = isinstance(out_shape, tuple)
    return pl.pallas_call(
        kernel,
        out_shape=out_shape,
        in_specs=[VMEM] * len(args),
        out_specs=[VMEM] * len(out_shape) if many else VMEM,
        scratch_shapes=scratch,
        compiler_params=pltpu.CompilerParams(vmem_limit_bytes=8 * MIB),
        cost_estimate=pl.CostEstimate(flops=1000, bytes_accessed=1000, transcendentals=0),
        name=name,
    )(*args)


def send_early_kernel(codes_ref, w_ref, acc_ref, send_ref, lhs, *, blocks, at):
    other = 1 - lax.axis_index("layer") // 2
    depth = lhs.shape[1]
    gather_rows(codes_ref, lhs, blocks, pl.ds(pl.multiple_of(other * depth, depth), depth))

    def body(c, n):
        cols = pl.ds(c, n)
        total = acc_ref[:, cols] + product(lhs, w_ref.at[other], at + c, n)
        send_ref[:, cols] = total.astype(BF16)

    over_tiles(0, send_ref.shape[1], body)


def send_early(codes, w, acc, part, at):
    n, wide = acc.shape
    return call_tiny(
        functools.partial(send_early_kernel, blocks=send_blocks(part), at=at),
        jax.ShapeDtypeStruct((n, wide), BF16),
        [pltpu.VMEM((n, codes.shape[1] // 2), BF16)],
        f"early{part}",
        codes,
        w,
        acc,
    )


def rows_kernel(codes_ref, w_ref, out_ref, lhs, *, blocks, at):
    gather_rows(codes_ref, lhs, blocks)

    def body(c, n):
        out_ref[:, pl.ds(c, n)] = product(lhs, w_ref, at + c, n).astype(out_ref.dtype)

    over_tiles(0, out_ref.shape[1], body)


def decode_rows(codes, w, blocks, at, wide, dtype, name):
    tokens, depth = codes.shape
    n = tokens // 2
    return call_tiny(
        functools.partial(rows_kernel, blocks=blocks, at=at),
        jax.ShapeDtypeStruct((n, wide), dtype),
        [pltpu.VMEM((n, depth), BF16)],
        name,
        codes,
        w,
    )


def merge_kernel(keep_ref, early_ref, late_ref, new_ref, send_ref):
    m = new_ref.shape[0]
    split = early_ref.shape[1]
    for got, cols in ((early_ref, pl.ds(0, split)), (late_ref, pl.ds(split, late_ref.shape[1]))):
        new_ref[:, cols] = keep_ref[:m, cols] + got[:m, :].astype(F32)
        send_ref[:, cols] = (keep_ref[m:, cols] + got[m:, :].astype(F32)).astype(BF16)


def merge(keep, early, late):
    n, wide = keep.shape
    return pl.pallas_call(
        merge_kernel,
        out_shape=(
            jax.ShapeDtypeStruct((n // 2, wide), F32),
            jax.ShapeDtypeStruct((n // 2, wide), BF16),
        ),
        in_specs=[VMEM] * 3,
        out_specs=[VMEM] * 2,
        compiler_params=pltpu.CompilerParams(vmem_limit_bytes=8 * MIB),
        cost_estimate=pl.CostEstimate(flops=1000, bytes_accessed=1000, transcendentals=0),
        name="merge",
    )(keep, early, late)


def shards(
    resid_halves,
    enc_weight,
    enc_bias,
    jump_threshold,
    dec_weight,
    dec_bias,
    clamp_rows,
    clamp_feats,
    clamp_slots,
    clamp_values,
):
    group = lax.axis_index("layer")
    me = lax.axis_index("lat")
    source, core = group // 2, group % 2
    tokens = resid_halves.shape[1]
    width = enc_weight.shape[2]
    hw = width // 2
    masks = jnp.array(block_masks(), jnp.int32)
    rows = tokens // masks.shape[0]

    keep, send = encode(resid_halves, enc_weight)
    recv = xor_swap(send, "layer", 1)

    row_token = (
        jnp.bitwise_xor(masks, me)[:, None] * rows + jnp.arange(rows, dtype=jnp.int32)[None, :]
    ).reshape(tokens)
    my_rows = lax.dynamic_index_in_dim(clamp_rows, source, 0, keepdims=False)
    my_pick = lax.dynamic_index_in_dim(
        clamp_feats * clamp_values.shape[0] + clamp_slots, source, 0, keepdims=False
    )
    row_hot = (my_rows[:, None] == row_token[None, :]).astype(F32)
    pick = jnp.dot(my_pick.astype(F32), row_hot, precision=lax.Precision.HIGHEST).astype(jnp.int32)
    feat, slot = pick // clamp_values.shape[0], pick % clamp_values.shape[0]
    slot_hot = slot[:, None] == jnp.arange(clamp_values.shape[0], dtype=jnp.int32)[None, :]
    value = jnp.sum(jnp.where(slot_hot, clamp_values[None, :], 0.0), axis=1)
    first = core * hw
    column = feat - me * width - first

    my_bias = lax.dynamic_slice(enc_bias, (source, first), (1, hw))
    my_thresh = lax.dynamic_slice(jump_threshold, (source, first), (1, hw))
    pre = keep + recv + my_bias
    ramp = jnp.clip((pre - my_thresh) / 0.25 + 1.0, 0.0, 1.0)
    hit = column[:, None] == jnp.arange(hw, dtype=jnp.int32)[None, :]
    own = jnp.where(hit, value[:, None], pre * ramp).astype(BF16)

    own_sib = xor_swap(own, "layer", 1)

    starts = [sum(PARTS[:p]) * LANES for p in range(STEPS)]
    spans = [(p, starts[p], EARLY[p] * LANES) for p in range(STEPS)]
    weights, accs = own_part(own, own_sib, dec_weight, spans)
    far, weights = lax.optimization_barrier((xor_swap(own, "layer", 2), weights))
    codes = assemble(own, own_sib, far, xor_swap(far, "layer", 1))

    last = [None] * STEPS

    def exchange(data, link):
        if last[link] is not None:
            data = lax.optimization_barrier((data, last[link]))[0]
        last[link] = xor_swap(data, "lat", LINKS[link])
        return last[link]

    early = [
        exchange(send_early(codes, weights, acc, p, at), p) for (p, at, _), acc in zip(spans, accs)
    ]
    sends = [
        decode_rows(codes, weights, send_blocks(p), at + wide, PARTS[p] * LANES - wide, BF16, f"late{p}")
        for p, at, wide in spans
    ]
    sends[:READY] = lax.optimization_barrier(tuple(sends[:READY]))
    late = [exchange(sends[p], p) for p in range(STEPS)]
    keeps = [
        decode_rows(codes, weights, keep_blocks(p), starts[p], PARTS[p] * LANES, F32, f"keep{p}")
        for p in range(STEPS)
    ]
    late[FIRST], *keeps[:KEPT] = lax.optimization_barrier((late[FIRST], *keeps[:KEPT]))
    kept, out = {}, {}
    for p in range(STEPS):
        kept[p], out[p] = merge(keeps[p], early[p], late[p])
    for i in range(1, STEPS):
        for p in range(STEPS):
            total = kept[p] + exchange(out[p], (p + i) % STEPS).astype(F32)
            m = total.shape[0] // 2
            kept[p] = total[:m] if i < STEPS - 1 else total
            out[p] = total[m:].astype(BF16)
    summed = jnp.concatenate([kept[p] for p in range(STEPS)], axis=1)
    return (summed + dec_bias).astype(BF16)[None]


def solution(mesh):
    return jax.shard_map(
        shards,
        mesh=mesh,
        in_specs=(
            P("layer", None, None),
            P("layer", None, "lat"),
            P(None, "lat"),
            P(None, "lat"),
            P("layer", None, "lat", None),
            P("layer", None),
            P(),
            P(),
            P(),
            P(),
        ),
        out_specs=P("layer", "lat", None),
        check_vma=False,
    )
```

```python
import functools

import jax
import jax.numpy as jnp
from jax import lax
from jax.experimental import pallas as pl
from jax.experimental.pallas import tpu as pltpu
from jax.sharding import PartitionSpec as P

BF16, F32 = jnp.bfloat16, jnp.float32
LINKS = (8, 1, 4, 24, 3)
STEPS = len(LINKS)
LANES, TILE = 128, 512
PARTS = (12, 13, 13, 13, 13)
EARLY = (6, 6, 6, 6, 6)
READY = 4
VMEM = pl.BlockSpec(memory_space=pltpu.VMEM)
HBM = pl.BlockSpec(memory_space=pltpu.HBM)
MIB = 1 << 20
COPIES = 4


def xor_swap(value, axis, mask):
    return lax.ppermute(value, axis, [(i, i ^ mask) for i in range(lax.axis_size(axis))])


def block_masks():
    n = 1 << STEPS
    out = []
    for j in range(n):
        m = 0
        for k in range(STEPS):
            if (j >> (STEPS - 1 - k)) & 1:
                m ^= LINKS[k]
        out.append(m)
    return out


def part_blocks(first):
    out = []
    for j in range(1 << STEPS):
        base = 0
        for i in range(STEPS):
            if (j >> (STEPS - 1 - i)) & 1:
                base |= 1 << (STEPS - 1 - (first + i) % STEPS)
        out.append(base)
    return out


def encode_kernel(
    x_hbm, w_hbm, keep_ref, send_ref, xbuf, wbuf, xsem, wsem, *, masks, rows, chunks
):
    me = lax.axis_index("lat")
    core = lax.axis_index("layer") % 2
    width = w_hbm.shape[2] // 2
    copies = []
    for k, (at, depth) in enumerate(chunks):
        ks = pl.ds(at, depth)
        mine = [pltpu.make_async_copy(w_hbm.at[0, ks], wbuf.at[ks], wsem.at[k])]
        for j, mask in enumerate(masks):
            src = pl.multiple_of(jnp.bitwise_xor(me, mask) * rows, rows)
            mine.append(
                pltpu.make_async_copy(
                    x_hbm.at[0, pl.ds(src, rows), ks],
                    xbuf.at[pl.ds(j * rows, rows), ks],
                    xsem.at[k * len(masks) + j],
                )
            )
        copies.append(mine)
    for mine in copies:
        for c in mine:
            c.start()
    half = (
        pl.ds(pl.multiple_of((1 - core) * width, width), width),
        pl.ds(pl.multiple_of(core * width, width), width),
    )
    for k, (at, depth) in enumerate(chunks):
        for c in copies[k]:
            c.wait()
        ks = pl.ds(at, depth)
        for ref, cols in zip((send_ref, keep_ref), half):
            d = jnp.dot(xbuf[:, ks], wbuf[ks, cols], preferred_element_type=F32)
            ref[...] = d if k == 0 else ref[...] + d


def encode(x, w):
    tokens, depth = x.shape[1], x.shape[2]
    width = w.shape[2] // 2
    masks = block_masks()
    rows = tokens // len(masks)
    q = depth // 4
    chunks = ((0, q), (q, 3 * q))
    half = pltpu.VMEM((tokens, width), F32)
    return pl.pallas_call(
        functools.partial(encode_kernel, masks=masks, rows=rows, chunks=chunks),
        out_shape=(half, half),
        in_specs=[HBM] * 2,
        out_specs=[VMEM] * 2,
        scratch_shapes=[
            pltpu.VMEM((tokens, depth), BF16),
            pltpu.VMEM((depth, 2 * width), BF16),
            pltpu.SemaphoreType.DMA((len(masks) * len(chunks),)),
            pltpu.SemaphoreType.DMA((len(chunks),)),
        ],
        compiler_params=pltpu.CompilerParams(vmem_limit_bytes=54 * MIB),
        cost_estimate=pl.CostEstimate(
            flops=4 * tokens * depth * width,
            bytes_accessed=2 * (tokens * depth + 2 * depth * width) + 8 * tokens * width,
            transcendentals=0,
        ),
        name="encode",
    )(x, w)


def copy_weights(dec_hbm, source, out_ref, sem, start):
    step = out_ref.shape[0] // COPIES
    for q in range(COPIES):
        at = pl.ds(q * step, step)
        c = pltpu.make_async_copy(dec_hbm.at[0, source, at], out_ref.at[at], sem.at[q])
        if start:
            c.start()
        else:
            c.wait()


def join_kernel(mine_ref, sib_ref, out_ref):
    core = lax.axis_index("layer") % 2
    hw = mine_ref.shape[1]
    out_ref[:, pl.ds(pl.multiple_of(core * hw, hw), hw)] = mine_ref[...]
    out_ref[:, pl.ds(pl.multiple_of((1 - core) * hw, hw), hw)] = sib_ref[...]


def assemble_kernel(own_ref, own_sib_ref, far_ref, far_sib_ref, out_ref):
    group = lax.axis_index("layer")
    source, core = group // 2, group % 2
    hw = own_ref.shape[1]
    for ref, s, c in (
        (own_ref, source, core),
        (own_sib_ref, source, 1 - core),
        (far_ref, 1 - source, core),
        (far_sib_ref, 1 - source, 1 - core),
    ):
        out_ref[:, pl.ds(pl.multiple_of((s * 2 + c) * hw, hw), hw)] = ref[...]


def assemble(*pieces):
    n, hw = pieces[0].shape
    return pl.pallas_call(
        assemble_kernel,
        out_shape=pltpu.VMEM((n, 4 * hw), BF16),
        in_specs=[VMEM] * 4,
        out_specs=VMEM,
        compiler_params=pltpu.CompilerParams(vmem_limit_bytes=8 * MIB),
        name="assemble",
    )(*pieces)


def gather_rows(codes_ref, lhs, blocks, cols=slice(None)):
    rows = lhs.shape[0] // len(blocks)
    for j, b in enumerate(blocks):
        lhs[pl.ds(j * rows, rows), :] = codes_ref[pl.ds(b * rows, rows), cols]


def over_tiles(begin, end, body):
    whole = (end - begin) // TILE

    @pl.loop(0, whole)
    def _(t):
        body(pl.multiple_of(begin + t * TILE, LANES), TILE)

    if begin + whole * TILE < end:
        body(begin + whole * TILE, end - begin - whole * TILE)


def product(lhs, w_ref, at, n):
    cols = pl.ds(pl.multiple_of(at, LANES), n)
    w = w_ref[:, cols] if len(w_ref.shape) == 2 else w_ref[:, :, cols].reshape(lhs.shape[1], n)
    return jnp.dot(lhs[...], w, preferred_element_type=F32)


def own_kernel(mine_ref, sib_ref, dec_hbm, *refs, spans):
    w_ref, *accs = refs[: 1 + len(spans)]
    codes, lhs, own_sem, far_sem = refs[1 + len(spans) :]
    source = lax.axis_index("layer") // 2
    own, far = w_ref.at[source], w_ref.at[1 - source]
    copy_weights(dec_hbm, source, own, own_sem, True)
    copy_weights(dec_hbm, 1 - source, far, far_sem, True)
    join_kernel(mine_ref, sib_ref, codes)
    copy_weights(dec_hbm, source, own, own_sem, False)
    for (part, at, wide), acc in zip(spans, accs):
        gather_rows(codes, lhs, send_blocks(part))

        def body(c, n):
            acc[:, pl.ds(c, n)] = product(lhs, own, at + c, n)

        over_tiles(0, wide, body)
    copy_weights(dec_hbm, 1 - source, far, far_sem, False)


def own_part(mine, sib, dec, spans):
    tokens, hw = mine.shape
    _, sources, depth, wide = dec.shape
    n = tokens // 2
    weights, *accs = pl.pallas_call(
        functools.partial(own_kernel, spans=spans),
        out_shape=[pltpu.VMEM((sources, depth, wide), BF16)]
        + [pltpu.VMEM((n, span[2]), F32) for span in spans],
        in_specs=[VMEM, VMEM, HBM],
        out_specs=[VMEM] * (1 + len(spans)),
        scratch_shapes=[pltpu.VMEM((tokens, depth), BF16), pltpu.VMEM((n, depth), BF16)]
        + [pltpu.SemaphoreType.DMA((COPIES,))] * 2,
        compiler_params=pltpu.CompilerParams(vmem_limit_bytes=14 * MIB),
        cost_estimate=pl.CostEstimate(
            flops=n * depth * wide, bytes_accessed=8 * depth * wide, transcendentals=0
        ),
        name="own",
    )(mine, sib, dec)
    return weights, accs


def send_blocks(part):
    blocks = part_blocks(part)
    return blocks[len(blocks) // 2 :]


def keep_blocks(part):
    blocks = part_blocks(part)
    return blocks[: len(blocks) // 2]


def call_tiny(kernel, out_shape, scratch, name, *args):
    many = isinstance(out_shape, tuple)
    return pl.pallas_call(
        kernel,
        out_shape=out_shape,
        in_specs=[VMEM] * len(args),
        out_specs=[VMEM] * len(out_shape) if many else VMEM,
        scratch_shapes=scratch,
        compiler_params=pltpu.CompilerParams(vmem_limit_bytes=8 * MIB),
        cost_estimate=pl.CostEstimate(flops=1000, bytes_accessed=1000, transcendentals=0),
        name=name,
    )(*args)


def send_early_kernel(codes_ref, w_ref, acc_ref, send_ref, lhs, *, blocks, at):
    other = 1 - lax.axis_index("layer") // 2
    depth = lhs.shape[1]
    gather_rows(codes_ref, lhs, blocks, pl.ds(pl.multiple_of(other * depth, depth), depth))

    def body(c, n):
        cols = pl.ds(c, n)
        total = acc_ref[:, cols] + product(lhs, w_ref.at[other], at + c, n)
        send_ref[:, cols] = total.astype(BF16)

    over_tiles(0, send_ref.shape[1], body)


def send_early(codes, w, acc, part, at):
    n, wide = acc.shape
    return call_tiny(
        functools.partial(send_early_kernel, blocks=send_blocks(part), at=at),
        jax.ShapeDtypeStruct((n, wide), BF16),
        [pltpu.VMEM((n, codes.shape[1] // 2), BF16)],
        f"early{part}",
        codes,
        w,
        acc,
    )


def rows_kernel(codes_ref, w_ref, out_ref, lhs, *, blocks, at):
    gather_rows(codes_ref, lhs, blocks)

    def body(c, n):
        out_ref[:, pl.ds(c, n)] = product(lhs, w_ref, at + c, n).astype(out_ref.dtype)

    over_tiles(0, out_ref.shape[1], body)


def decode_rows(codes, w, blocks, at, wide, dtype, name):
    tokens, depth = codes.shape
    n = tokens // 2
    return call_tiny(
        functools.partial(rows_kernel, blocks=blocks, at=at),
        jax.ShapeDtypeStruct((n, wide), dtype),
        [pltpu.VMEM((n, depth), BF16)],
        name,
        codes,
        w,
    )


def merge_kernel(keep_ref, early_ref, late_ref, new_ref, send_ref):
    m = new_ref.shape[0]
    split = early_ref.shape[1]
    for got, cols in ((early_ref, pl.ds(0, split)), (late_ref, pl.ds(split, late_ref.shape[1]))):
        new_ref[:, cols] = keep_ref[:m, cols] + got[:m, :].astype(F32)
        send_ref[:, cols] = (keep_ref[m:, cols] + got[m:, :].astype(F32)).astype(BF16)


def merge(keep, early, late):
    n, wide = keep.shape
    return pl.pallas_call(
        merge_kernel,
        out_shape=(
            jax.ShapeDtypeStruct((n // 2, wide), F32),
            jax.ShapeDtypeStruct((n // 2, wide), BF16),
        ),
        in_specs=[VMEM] * 3,
        out_specs=[VMEM] * 2,
        compiler_params=pltpu.CompilerParams(vmem_limit_bytes=8 * MIB),
        cost_estimate=pl.CostEstimate(flops=1000, bytes_accessed=1000, transcendentals=0),
        name="merge",
    )(keep, early, late)


def shards(
    resid_halves,
    enc_weight,
    enc_bias,
    jump_threshold,
    dec_weight,
    dec_bias,
    clamp_rows,
    clamp_feats,
    clamp_slots,
    clamp_values,
):
    group = lax.axis_index("layer")
    me = lax.axis_index("lat")
    source, core = group // 2, group % 2
    tokens = resid_halves.shape[1]
    width = enc_weight.shape[2]
    hw = width // 2
    masks = jnp.array(block_masks(), jnp.int32)
    rows = tokens // masks.shape[0]

    keep, send = encode(resid_halves, enc_weight)
    recv = xor_swap(send, "layer", 1)

    row_token = (
        jnp.bitwise_xor(masks, me)[:, None] * rows + jnp.arange(rows, dtype=jnp.int32)[None, :]
    ).reshape(tokens)
    my_rows = lax.dynamic_index_in_dim(clamp_rows, source, 0, keepdims=False)
    my_pick = lax.dynamic_index_in_dim(
        clamp_feats * clamp_values.shape[0] + clamp_slots, source, 0, keepdims=False
    )
    row_hot = (my_rows[:, None] == row_token[None, :]).astype(F32)
    pick = jnp.dot(my_pick.astype(F32), row_hot, precision=lax.Precision.HIGHEST).astype(jnp.int32)
    feat, slot = pick // clamp_values.shape[0], pick % clamp_values.shape[0]
    slot_hot = slot[:, None] == jnp.arange(clamp_values.shape[0], dtype=jnp.int32)[None, :]
    value = jnp.sum(jnp.where(slot_hot, clamp_values[None, :], 0.0), axis=1)
    first = core * hw
    column = feat - me * width - first

    my_bias = lax.dynamic_slice(enc_bias, (source, first), (1, hw))
    my_thresh = lax.dynamic_slice(jump_threshold, (source, first), (1, hw))
    pre = keep + recv + my_bias
    ramp = jnp.clip((pre - my_thresh) / 0.25 + 1.0, 0.0, 1.0)
    hit = column[:, None] == jnp.arange(hw, dtype=jnp.int32)[None, :]
    own = jnp.where(hit, value[:, None], pre * ramp).astype(BF16)

    own_sib = xor_swap(own, "layer", 1)

    starts = [sum(PARTS[:p]) * LANES for p in range(STEPS)]
    spans = [(p, starts[p], EARLY[p] * LANES) for p in range(STEPS)]
    weights, accs = own_part(own, own_sib, dec_weight, spans)
    far, weights = lax.optimization_barrier((xor_swap(own, "layer", 2), weights))
    codes = assemble(own, own_sib, far, xor_swap(far, "layer", 1))

    last = [None] * STEPS

    def exchange(data, link):
        if last[link] is not None:
            data = lax.optimization_barrier((data, last[link]))[0]
        last[link] = xor_swap(data, "lat", LINKS[link])
        return last[link]

    early = [
        exchange(send_early(codes, weights, acc, p, at), p) for (p, at, _), acc in zip(spans, accs)
    ]
    sends = [
        decode_rows(codes, weights, send_blocks(p), at + wide, PARTS[p] * LANES - wide, BF16, f"late{p}")
        for p, at, wide in spans
    ]
    sends[:READY] = lax.optimization_barrier(tuple(sends[:READY]))
    late = [exchange(sends[p], p) for p in range(STEPS)]
    keeps = [
        decode_rows(codes, weights, keep_blocks(p), starts[p], PARTS[p] * LANES, F32, f"keep{p}")
        for p in range(STEPS)
    ]
    late[0], *keeps[:READY] = lax.optimization_barrier((late[0], *keeps[:READY]))
    kept, out = {}, {}
    for p in range(STEPS):
        kept[p], out[p] = merge(keeps[p], early[p], late[p])
    for i in range(1, STEPS):
        for p in range(STEPS):
            total = kept[p] + exchange(out[p], (p + i) % STEPS).astype(F32)
            m = total.shape[0] // 2
            kept[p] = total[:m] if i < STEPS - 1 else total
            out[p] = total[m:].astype(BF16)
    summed = jnp.concatenate([kept[p] for p in range(STEPS)], axis=1)
    return (summed + dec_bias).astype(BF16)[None]


def solution(mesh):
    return jax.shard_map(
        shards,
        mesh=mesh,
        in_specs=(
            P("layer", None, None),
            P("layer", None, "lat"),
            P(None, "lat"),
            P(None, "lat"),
            P("layer", None, "lat", None),
            P("layer", None),
            P(),
            P(),
            P(),
            P(),
        ),
        out_specs=P("layer", "lat", None),
        check_vma=False,
    )
```
